128 devices in a mesh: sec: 2 (over core), dev: 64 (over z, x, y).
Axes of the slice: x: 4, y: 4, z: 4, core: 2. Of those that a mesh axis runs over, the one named last changes fastest.
Arguments:
- tokens: bfloat16 [2048, 3584], P(('sec', 'dev')), may hold values from -6 to 6
- routes: int32 [2048, 8], P(('sec', 'dev')), may hold values from 0 to 127, all different within a row; in each aligned block of 16 rows (0 to 15, 16 to 31, ...) at most 2 rows name the same one
- gate_num: int32 [2048, 8], P(('sec', 'dev')), may hold values from 1 to 32
- w_gate: bfloat16 [128, 3584, 1024], P(('sec', 'dev')), may hold values from -0.09375 to 0.09375
- w_up: bfloat16 [128, 3584, 1024], P(('sec', 'dev')), may hold values from -0.09375 to 0.09375
- w_down: bfloat16 [128, 1024, 3584], P(('sec', 'dev')), may hold values from -0.1875 to 0.1875
- attn_gain: float32 [3584], replicated, may hold values from 0.25 to 1.75
- w_latent: bfloat16 [3584, 576], P('dev'), may hold values from -0.09375 to 0.09375
- kv_gain: float32 [512], replicated, may hold values from 0.25 to 1.75
- queries: bfloat16 [2048, 64, 576], P(('sec', 'dev')), may hold values from -9 to 9
- cache_pool: bfloat16 [4096, 64, 576], P(('sec', 'dev')), may hold values from -4 to 4
- block_table: int32 [2048, 4], P(('sec', 'dev')), may hold values from 0 to 31
- lengths: int32 [128, 16], P(('sec', 'dev')), may hold values from 1 to 256, 2048 in all within a row
Outputs:
- layer_out: bfloat16 [2048, 3584], P(('sec', 'dev'))
- new_latent: bfloat16 [2048, 576], P(('sec', 'dev'))
- context: bfloat16 [2048, 32768], P(('sec', 'dev'))
The draws below stay inside these ranges and needn't reach their ends.
Inputs may be any that keep to these rules, and one draw needn't show every extreme that they name: `routes`: in each aligned block of 16 rows (the rows of one device) no expert is named by more than 2 rows. `block_table`: each device's rows point only into that device's 32 pages; pages may be shared by rows. The 16 lengths of one device add up to 2048.
All inputs are finite; a program needn't handle non-finite values.
Results may differ from the reference program's by a relative error of at most 0.0064.
Values may be sent and summed in bfloat16 or wider, within the bound.
A program may use at most 128 MiB of HBM per device.

```python
import math
import jax
import jax.numpy as jnp
import numpy as np
from jax import lax

D = 3584
HID = 1024
HEADS = 64
LAT = 512
ROPE = 64
TOP = 8
GATE_DEN = 32
PAGE = 64
MAXP = 4
POOL = 32
TOK_DEV = 16
KDIM = 576
MAXLEN = 256
EXPERTS = 128
CAP = 2
TOKENS = 2048
POOL_ALL = 4096
N_SEC = 2
N_DEV = 64


def draw_queries(key, part):
    base = jax.random.truncated_normal(jax.random.fold_in(key, 11), -4.0, 4.0, (TOKENS, HEADS, LAT + ROPE), jnp.float32)
    return base.astype(jnp.bfloat16)


def draw_cache_pool(key, part):
    shape = (POOL_ALL, PAGE, LAT + ROPE)
    base = jax.random.truncated_normal(jax.random.fold_in(key, 21), -4.0, 4.0, shape, jnp.float32)
    return base.astype(jnp.bfloat16)


def plant(drawn, own_key, smallest, largest):
    index_at = [jax.random.randint(jax.random.fold_in(own_key, axis), (), 0, length) for axis, length in enumerate(drawn.shape)]
    widest = drawn.shape.index(max(drawn.shape))
    next_to = index_at[:widest] + [(index_at[widest] + 1) % drawn.shape[widest]] + index_at[widest + 1:]
    return drawn.at[tuple(index_at)].set(smallest).at[tuple(next_to)].set(largest)


def steps_of(stream_key, dims, pieces, least, largest):
    loudness, own = 1.0, jax.random.fold_in(stream_key, 6)
    for dim, shards_of in pieces:
        heights = jnp.exp(jax.random.uniform(jax.random.fold_in(own, dim), (shards_of,), jnp.float32, least / len(pieces), largest / len(pieces)))
        loudness = loudness * jnp.repeat(heights, dims[dim] // shards_of).reshape([-1 if axis == dim else 1 for axis in range(len(dims))])
    return loudness


def length_profile(number_of, total, limit, lean):
    weights = [(1 << 20) // math.isqrt(standing ** lean) + 1 for standing in range(2, number_of + 1)]
    spare, given = total - limit - (number_of - 1), [1] * (number_of - 1)
    while spare > 0:
        movable = [i for i in range(number_of - 1) if given[i] < limit]
        mass, left = sum([weights[i] for i in movable]), spare
        for i in movable:
            extra = min(limit - given[i], max(1, left * weights[i] // mass), spare)
            given[i] = given[i] + extra
            spare = spare - extra
    return np.array([limit] + given)


def ragged(stream_key, count, total, reach, slope):
    if count == 2:
        one = jax.random.randint(stream_key, (), max(1, total - reach), min(reach, total - 1) + 1)
        return jnp.stack([one, total - one])
    sizes = jnp.asarray(length_profile(count, total, reach, slope), jnp.int32)
    couples = (count - 1) // 2
    donor, taker = sizes[1:1 + 2 * couples:2], sizes[2:2 + 2 * couples:2]
    margin = jnp.minimum(donor - 1, reach - taker)
    passed = jax.random.randint(jax.random.fold_in(stream_key, 1), (couples,), 0, 1 << 20) % (margin + 1)
    sizes = sizes.at[1:1 + 2 * couples:2].set(donor - passed).at[2:2 + 2 * couples:2].set(taker + passed)
    return sizes[jax.random.permutation(jax.random.fold_in(stream_key, 2), count)]


def assign_block(own_key, own, number, rows, count, top, bound, slope):
    order = jax.random.permutation(own_key, count)
    heavy_load, usual = shares(count, rows * top, bound, slope, True), shares(count, rows * top, bound, slope, False)
    places = jnp.arange(count)

    def named(sizes, offset_by):
        used = int((sizes > 0).sum())
        fixed = max(1, used // 4)
        passed = fixed + (places - fixed + offset_by * (used - fixed)) % max(1, count - fixed)
        return jnp.zeros((count,), jnp.int32).at[order[jnp.where(places < fixed, places, passed)]].set(jnp.asarray(sizes, jnp.int32))

    sizes = jnp.where(number % 4 == 0, named(heavy_load, number // 4), named(usual, number - number // 4 - 1))
    mixed = jax.random.permutation(jax.random.fold_in(own, 3), count)
    source_of, taker = mixed[0:count // 2 * 2:2], mixed[1:count // 2 * 2:2]
    room = jnp.minimum(sizes[source_of] - 1, bound - sizes[taker]) // 2
    room = jnp.where((source_of == order[0]) | (taker == order[0]) | (sizes[taker] == 0), 0, jnp.maximum(room, 0))
    passed = jax.random.randint(jax.random.fold_in(own, 4), (count // 2,), 0, 1 << 20) % (room + 1)
    sizes = sizes.at[source_of].add(-passed).at[taker].add(passed)
    members = jnp.searchsorted(jnp.cumsum(sizes), jnp.arange(rows * top), side="right").astype(jnp.int32)
    listing = members.reshape(top, rows).T
    listing = listing[jax.random.permutation(jax.random.fold_in(own, 1), rows)]
    offset_by = jax.random.randint(jax.random.fold_in(own, 2), (rows, 1), 0, top)
    return jnp.take_along_axis(listing, (jnp.arange(top)[None, :] + offset_by) % top, axis=1)


def shares(amount, total, bound, lean, full):
    weights = [(1 << 20) // math.isqrt(standing ** lean) + 1 for standing in range(1, amount + 1)]
    largest = bound if full else min(bound, max(-(-total // amount), total * weights[0] // sum(weights)))
    least = 1 if total - largest >= amount - 1 else 0
    holding, spare = [largest] + [least] * (amount - 1), total - largest - least * (amount - 1)
    while spare > 0:
        candidates = [i for i in range(1, amount) if holding[i] < largest] or [i for i in range(1, amount) if holding[i] < bound]
        whole, left = sum([weights[i] for i in candidates]), spare
        for i in candidates:
            extra = min(bound - holding[i], max(1, left * weights[i] // whole), spare)
            holding[i] = holding[i] + extra
            spare = spare - extra
    return np.array(holding)


def scatter_about(rng, shape, scale, bound, shards=(), kind=jnp.bfloat16):
    level = steps_of(rng, shape, shards, -0.22, 0.18) if shards else 1.0
    array = jax.random.normal(rng, shape, jnp.float32) * scale * level
    return jnp.minimum(jnp.maximum(array, -bound), bound).astype(kind)


def setup_inputs(seed: int = 0) -> dict:
    seeds = jax.random.split(jax.random.key(seed), 14)
    tokens = scatter_about(seeds[0], (TOKENS, D), 1.0, 6.0, ((0, 128),))
    routes_keys = jax.random.split(jax.random.fold_in(seeds[1], 1), TOKENS // TOK_DEV)
    routes_turns = jax.random.permutation(jax.random.fold_in(seeds[1], 3), TOKENS // TOK_DEV)
    routes = jax.vmap(lambda own, number: assign_block(jax.random.fold_in(seeds[1], 2), own, number, TOK_DEV, EXPERTS, TOP, CAP, 2))(routes_keys, routes_turns).reshape((TOKENS, TOP))
    gate_num = plant(jax.random.randint(seeds[2], (TOKENS, TOP), 1, 33), jax.random.fold_in(seeds[2], 1), 1, 32).astype(jnp.int32)
    w_gate = scatter_about(seeds[3], (EXPERTS, D, HID), D ** -0.5, 0.09375, ((0, 128),))
    w_up = scatter_about(seeds[4], (EXPERTS, D, HID), D ** -0.5, 0.09375, ((0, 128),))
    w_down = scatter_about(seeds[5], (EXPERTS, HID, D), HID ** -0.5, 0.1875, ((0, 128),))
    attn_gain = jnp.clip(1.0 + 0.15 * jax.random.normal(seeds[6], (D,), jnp.float32), 0.25, 1.75)
    w_latent = scatter_about(seeds[7], (D, KDIM), D ** -0.5, 0.09375, ((0, 64),))
    kv_gain = jnp.clip(1.0 + 0.15 * jax.random.normal(seeds[8], (LAT,), jnp.float32), 0.25, 1.75)
    queries = draw_queries(jax.random.fold_in(seeds[13], 71), 0)
    cache_pool = draw_cache_pool(jax.random.fold_in(seeds[13], 71), 0)
    block_table = plant(jax.random.randint(seeds[11], (TOKENS, MAXP), 0, POOL), jax.random.fold_in(seeds[11], 1), 0, POOL - 1).astype(jnp.int32)
    lengths = jax.vmap(lambda own: ragged(own, TOK_DEV, TOK_DEV * MAXLEN // 2, MAXLEN, 2))(jax.random.split(seeds[12], (N_SEC * N_DEV))).reshape((N_SEC * N_DEV, TOK_DEV)).astype(jnp.int32)
    return {"tokens": tokens, "routes": routes, "gate_num": gate_num, "w_gate": w_gate, "w_up": w_up, "w_down": w_down, "attn_gain": attn_gain, "w_latent": w_latent, "kv_gain": kv_gain, "queries": queries, "cache_pool": cache_pool, "block_table": block_table, "lengths": lengths}


score_scale = 192.0 ** (-0.5)
norm_eps = 1e-06

def slot_numbers(expert_rows):
    onehot = (expert_rows[:, None] == jnp.arange(EXPERTS, dtype=jnp.int32)[None, :]).astype(jnp.int32)
    before = jnp.cumsum(onehot, axis=0) - onehot
    return lax.optimization_barrier(jnp.sum(before * onehot, axis=1)).astype(jnp.int32)

def rms_scale(values, gain):
    mean_square = lax.optimization_barrier(jnp.mean(values * values, axis=-1, keepdims=True))
    return values * lax.rsqrt(mean_square + norm_eps) * gain.astype(jnp.float32)

def expert_apply(rows, gates, gate_proj, up_proj, down_proj):
    gate_part = jnp.dot(rows, gate_proj, preferred_element_type=jnp.float32)
    up_part = jnp.dot(rows, up_proj, preferred_element_type=jnp.float32)
    hidden = (jax.nn.silu(gate_part) * up_part).astype(jnp.bfloat16)
    result = jnp.dot(hidden, down_proj, preferred_element_type=jnp.float32)
    return (result * gates.astype(jnp.float32)[:, None]).astype(jnp.bfloat16)

def attend(queries, key_rows, row_lengths):
    span = key_rows.shape[1] - 1
    kept = jnp.concatenate([jnp.arange(span, dtype=jnp.int32)[None, :] < row_lengths[:, None], jnp.ones((key_rows.shape[0], 1), dtype=bool)], axis=1)
    scores = jnp.einsum('thk,tpk->thp', queries.astype(jnp.float32), key_rows.astype(jnp.float32)) * score_scale
    scores = jnp.where(kept[:, None, :], scores, -1e+30)
    top_score = lax.optimization_barrier(jnp.max(scores, axis=2, keepdims=True))
    raised = jnp.exp(scores - top_score)
    probs = (raised / lax.optimization_barrier(jnp.sum(raised, axis=2, keepdims=True))).astype(jnp.bfloat16)
    values = key_rows[:, :, :LAT]
    mixed = jnp.einsum('thp,tpl->thl', probs.astype(jnp.float32), values.astype(jnp.float32))
    return mixed.astype(jnp.bfloat16).reshape(key_rows.shape[0], HEADS * LAT)

def reference(tokens, routes, gate_num, w_gate, w_up, w_down, attn_gain, w_latent, kv_gain, queries, cache_pool, block_table, lengths):
    device_count = N_SEC * N_DEV
    rows_dev = TOK_DEV * TOP
    expert_rows = routes.reshape(device_count, rows_dev).astype(jnp.int32)
    slots = jax.vmap(slot_numbers)(expert_rows)
    source = jnp.arange(device_count, dtype=jnp.int32)[:, None]
    column = (source * CAP + slots).astype(jnp.int32)
    row_ids = jnp.arange(device_count * rows_dev, dtype=jnp.int32).reshape(device_count, rows_dev)
    table = jnp.zeros((EXPERTS, device_count * CAP), jnp.int32).at[expert_rows, column].set(row_ids + 1)
    gate_flat = gate_num.reshape(-1).astype(jnp.float32) / GATE_DEN

    def one_expert(packed):
        filled, gate_proj, up_proj, down_proj = packed
        live_slot = filled > 0
        source_row = jnp.maximum(filled - 1, 0)
        rows = jnp.where(live_slot[:, None], tokens[source_row // TOP], jnp.zeros((), tokens.dtype))
        gates = jnp.where(live_slot, gate_flat[source_row], 0.0)
        return expert_apply(rows, gates, gate_proj, up_proj, down_proj)
    outputs = lax.map(one_expert, (table, w_gate, w_up, w_down))
    picked = outputs[expert_rows.reshape(-1), column.reshape(-1)]
    moe = lax.optimization_barrier(jnp.sum(picked.astype(jnp.float32).reshape(TOKENS, TOP, D), axis=1))
    layer_out = (tokens.astype(jnp.float32) + moe).astype(jnp.bfloat16)
    normed = rms_scale(layer_out.astype(jnp.float32), attn_gain).astype(jnp.bfloat16)
    latent_full = jnp.dot(normed, w_latent, preferred_element_type=jnp.float32)
    latent = rms_scale(latent_full[:, :LAT], kv_gain)
    new_latent = jnp.concatenate([latent, latent_full[:, LAT:]], axis=1).astype(jnp.bfloat16)
    pool = cache_pool.reshape(device_count, POOL, PAGE, KDIM)

    def one_device(packed):
        device_queries, pages, table_rows, row_lengths, own = packed
        key_rows = pages[table_rows].reshape(TOK_DEV, MAXLEN, KDIM)
        key_rows = jnp.concatenate([key_rows, own[:, None, :]], axis=1)
        return attend(device_queries, key_rows, row_lengths)
    context = lax.map(one_device, (queries.reshape(device_count, TOK_DEV, HEADS, KDIM), pool, block_table.reshape(device_count, TOK_DEV, MAXP).astype(jnp.int32), lengths.astype(jnp.int32), new_latent.reshape(device_count, TOK_DEV, KDIM)))
    context = context.reshape(TOKENS, HEADS * LAT)
    return (layer_out, new_latent, context)
```

```python
import functools

import jax
import jax.numpy as jnp
from jax import lax
from jax.experimental import pallas as pl
from jax.experimental.pallas import tpu as pltpu
from jax.sharding import PartitionSpec as P

MESH = pl.DeviceIdType.MESH
GATE_DEN = 32
CAP = 2
SIDE = 4
score_scale = 192.0 ** (-0.5)
norm_eps = 1e-06
CHUNKS = 4


def rms_scale(values, gain):
    mean_square = jnp.mean(values * values, axis=-1, keepdims=True)
    return values * lax.rsqrt(mean_square + norm_eps) * gain


def place():
    sec, dev = lax.axis_index("sec"), lax.axis_index("dev")
    z = lax.div(dev, SIDE * SIDE)
    x = lax.rem(lax.div(dev, SIDE), SIDE)
    y = lax.rem(dev, SIDE)
    return sec, z, x, y


def partner(here, part, i, back):
    sec, z, x, y = here
    ds, dz, dx = lax.rem(i, 2), lax.rem(lax.div(i, 2), SIDE), lax.div(i, 2 * SIDE)
    dy = lax.rem(part + 2 * SIDE - dz - dx, SIDE)
    if back:
        dz, dx, dy = SIDE - dz, SIDE - dx, SIDE - dy
    return (
        lax.rem(sec + ds, 2),
        lax.rem(z + dz, SIDE) * SIDE * SIDE + lax.rem(x + dx, SIDE) * SIDE + lax.rem(y + dy, SIDE),
    )


def moe_kernel(
    peers,
    tok_ref,
    routes_ref,
    gate_ref,
    w_gate,
    w_up,
    w_down,
    out_ref,
    sent,
    got,
    served,
    back,
    wg,
    wu,
    wd,
    hid,
    rows_buf,
    w_sem,
    sent_sem,
    got_sem,
    served_sem,
    back_sem,
):
    here = place()
    sec, z, x, y = here
    tok_rows, width = tok_ref.shape
    parts = got_sem.shape[0]
    per_part = peers // parts
    quarter = peers // SIDE

    barrier = pltpu.get_barrier_semaphore()

    for q in range(SIDE):

        def greet(i, c, q=q):
            pl.semaphore_signal(barrier, inc=1, device_id=partner(here, q, i, False), device_id_type=MESH)
            return c

        lax.fori_loop(1 if q == 0 else 0, quarter, greet, 0)

    loads = [
        pltpu.make_async_copy(src.at[0], dst, w_sem.at[n])
        for n, (src, dst) in enumerate(((w_gate, wg), (w_up, wu), (w_down, wd)))
    ]
    for load in loads:
        load.start()

    row = lax.broadcasted_iota(jnp.int32, (1, peers * CAP), 1)
    j, c = row >> 1, row & 1
    ds, dz, dx, part = j & 1, (j >> 1) & 3, (j >> 3) & 3, j >> 5
    dy = (part - dz - dx) & 3
    expert = ((sec + ds) & 1) * (peers // 2) + ((z + dz) & 3) * 16 + ((x + dx) & 3) * 4 + ((y + dy) & 3)
    named = jnp.zeros((tok_rows, peers * CAP), jnp.float32)
    gates = jnp.zeros((tok_rows, peers * CAP), jnp.float32)
    for k in range(routes_ref.shape[1]):
        hit = routes_ref[:, k : k + 1] == expert
        named = jnp.where(hit, 1.0, named)
        gates = jnp.where(hit, gate_ref[:, k : k + 1].astype(jnp.float32), gates)
    earlier = (
        lax.broadcasted_iota(jnp.int32, (tok_rows, tok_rows), 1)
        < lax.broadcasted_iota(jnp.int32, (tok_rows, tok_rows), 0)
    ).astype(jnp.float32)
    before = jnp.dot(earlier, named, preferred_element_type=jnp.float32)
    here_slot = before == c.astype(jnp.float32)
    pick = jnp.where(here_slot, named, 0.0).astype(jnp.bfloat16)
    weigh = (jnp.where(here_slot, gates, 0.0) * (1.0 / GATE_DEN)).astype(jnp.bfloat16)

    rows_q = quarter * CAP
    for q in range(SIDE):
        gathered = lax.dot_general(
            pick[:, q * rows_q : (q + 1) * rows_q],
            tok_ref[...],
            (((0,), (0,)), ((), ())),
            preferred_element_type=jnp.float32,
        ).astype(jnp.bfloat16)
        sent[q * quarter : (q + 1) * quarter] = gathered.reshape(quarter, CAP, width)

    pl.semaphore_wait(barrier, peers - 1)

    def exchange(src, dst, src_sem, dst_sem, q, reverse):
        def go(i, c):
            n = q * quarter + i
            pltpu.make_async_remote_copy(
                src_ref=src.at[n],
                dst_ref=dst.at[n],
                send_sem=src_sem,
                recv_sem=dst_sem,
                device_id=partner(here, q, i, reverse),
                device_id_type=MESH,
            ).start()
            return c

        if q == 0:
            pltpu.make_async_copy(src.at[0], dst.at[0], dst_sem).start()
        lax.fori_loop(1 if q == 0 else 0, quarter, go, 0)

    def arrived(dst, sem, lo, n):
        view = dst.at[pl.ds(lo, n)]
        pltpu.make_async_copy(view, view, sem).wait()

    for q in range(SIDE):
        exchange(sent, got, sent_sem, got_sem.at[q * parts // SIDE], q, False)

    for n, load in enumerate(loads):
        load.wait()

    hidden = wg.shape[1]
    tile_h, tile_o = 256, 512
    for p in range(parts):
        arrived(got, got_sem.at[p], p * per_part, per_part)
        rows_buf[...] = got[p * per_part : (p + 1) * per_part].reshape(per_part * CAP, width)

        def up(n, c):
            cols = pl.ds(pl.multiple_of(n * tile_h, tile_h), tile_h)
            g = jnp.dot(rows_buf[...], wg[:, cols], preferred_element_type=jnp.float32)
            u = jnp.dot(rows_buf[...], wu[:, cols], preferred_element_type=jnp.float32)
            hid[:, cols] = (g / (1.0 + jnp.exp(-g)) * u).astype(jnp.bfloat16)
            return c

        lax.fori_loop(0, hidden // tile_h, up, 0)

        def down(n, c, p=p):
            cols = pl.ds(pl.multiple_of(n * tile_o, tile_o), tile_o)
            o = jnp.dot(hid[...], wd[:, cols], preferred_element_type=jnp.float32)
            served[p * per_part : (p + 1) * per_part, :, cols] = o.astype(jnp.bfloat16).reshape(
                per_part, CAP, tile_o
            )
            return c

        lax.fori_loop(0, width // tile_o, down, 0)
        for q in range(p * SIDE // parts, (p + 1) * SIDE // parts):
            exchange(served, back, served_sem, back_sem, q, True)

    arrived(back, back_sem, 0, peers)
    total = tok_ref[...].astype(jnp.float32)
    for q in range(SIDE):
        piece = back[q * quarter : (q + 1) * quarter].reshape(rows_q, width)
        total += jnp.dot(weigh[:, q * rows_q : (q + 1) * rows_q], piece, preferred_element_type=jnp.float32)
    out_ref[...] = total.astype(jnp.bfloat16)

    arrived(sent, sent_sem, 1, peers - 1)
    arrived(served, served_sem, 1, peers - 1)


def moe(tokens, routes, gate_num, w_gate, w_up, w_down, peers):
    tok_rows, width = tokens.shape
    hidden = w_gate.shape[2]
    slots = pltpu.VMEM((peers, CAP, width), jnp.bfloat16)
    rows = peers * CAP // CHUNKS
    dma = pltpu.SemaphoreType.DMA
    return pl.pallas_call(
        functools.partial(moe_kernel, peers),
        out_shape=jax.ShapeDtypeStruct((tok_rows, width), jnp.bfloat16),
        in_specs=[pl.BlockSpec(memory_space=pltpu.VMEM)] * 3 + [pl.BlockSpec(memory_space=pl.ANY)] * 3,
        out_specs=pl.BlockSpec(memory_space=pltpu.VMEM),
        scratch_shapes=[
            slots,
            slots,
            slots,
            slots,
            pltpu.VMEM((width, hidden), jnp.bfloat16),
            pltpu.VMEM((width, hidden), jnp.bfloat16),
            pltpu.VMEM((hidden, width), jnp.bfloat16),
            pltpu.VMEM((rows, hidden), jnp.bfloat16),
            pltpu.VMEM((rows, width), jnp.bfloat16),
            dma((3,)),
            dma,
            dma((CHUNKS,)),
            dma,
            dma,
        ],
        compiler_params=pltpu.CompilerParams(
            collective_id=0, has_side_effects=True, vmem_limit_bytes=56 << 20
        ),
    )(tokens, routes, gate_num, w_gate, w_up, w_down)


def per_device(
    tokens,
    routes,
    gate_num,
    w_gate,
    w_up,
    w_down,
    attn_gain,
    w_latent,
    kv_gain,
    queries,
    cache_pool,
    block_table,
    lengths,
):
    peers = lax.axis_size("sec") * lax.axis_size("dev")
    tok_rows, width = tokens.shape
    layer_out = moe(tokens, routes, gate_num, w_gate, w_up, w_down, peers)
    normed = rms_scale(layer_out.astype(jnp.float32), attn_gain).astype(jnp.bfloat16)
    kdim = w_latent.shape[1]
    lat_width = kv_gain.shape[0]
    latent_full = jnp.dot(
        normed,
        lax.all_gather(w_latent, "dev", axis=0, tiled=True),
        preferred_element_type=jnp.float32,
    )
    latent = rms_scale(latent_full[:, :lat_width], kv_gain)
    new_latent = jnp.concatenate([latent, latent_full[:, lat_width:]], axis=1).astype(jnp.bfloat16)
    page_rows = cache_pool[block_table]
    key_rows = jnp.concatenate(
        [page_rows.reshape(tok_rows, -1, kdim), new_latent[:, None, :]], axis=1
    )
    span = key_rows.shape[1] - 1
    row_lengths = lengths.reshape(-1)
    kept = jnp.concatenate(
        [
            jnp.arange(span, dtype=jnp.int32)[None, :] < row_lengths[:, None],
            jnp.ones((tok_rows, 1), dtype=bool),
        ],
        axis=1,
    )
    scores = (
        jnp.einsum("thk,tpk->thp", queries, key_rows, preferred_element_type=jnp.float32)
        * score_scale
    )
    scores = jnp.where(kept[:, None, :], scores, -1e30)
    top_score = jnp.max(scores, axis=2, keepdims=True)
    raised = jnp.exp(scores - top_score)
    probs = (raised / jnp.sum(raised, axis=2, keepdims=True)).astype(jnp.bfloat16)
    mixed = jnp.einsum(
        "thp,tpl->thl", probs, key_rows[:, :, :lat_width], preferred_element_type=jnp.float32
    )
    context = mixed.astype(jnp.bfloat16).reshape(tok_rows, -1)
    return (layer_out, new_latent, context)


def solution(mesh):
    both = ("sec", "dev")
    return jax.shard_map(
        per_device,
        mesh=mesh,
        in_specs=(
            P(both, None),
            P(both, None),
            P(both, None),
            P(both, None, None),
            P(both, None, None),
            P(both, None, None),
            P(),
            P("dev", None),
            P(),
            P(both, None, None),
            P(both, None, None),
            P(both, None),
            P(both, None),
        ),
        out_specs=(P(both, None), P(both, None), P(both, None)),
        check_vma=False,
    )
```

```python
import functools

import jax
import jax.numpy as jnp
from jax import lax
from jax.experimental import pallas as pl
from jax.experimental.pallas import tpu as pltpu
from jax.sharding import PartitionSpec as P

MESH = pl.DeviceIdType.MESH
GATE_DEN = 32
CAP = 2
SIDE = 4
score_scale = 192.0 ** (-0.5)
norm_eps = 1e-06
CHUNKS = 4
LANE_TILES = 2


def rms_scale(values, gain):
    mean_square = jnp.mean(values * values, axis=-1, keepdims=True)
    return values * lax.rsqrt(mean_square + norm_eps) * gain


def place():
    sec, dev = lax.axis_index("sec"), lax.axis_index("dev")
    z = lax.div(dev, SIDE * SIDE)
    x = lax.rem(lax.div(dev, SIDE), SIDE)
    y = lax.rem(dev, SIDE)
    return sec, z, x, y


def offsets(parts):
    listed = []
    for part in range(parts):
        for i in range(2 * SIDE * SIDE):
            ds, dz, dx = i % 2, i // 2 % SIDE, i // (2 * SIDE)
            listed.append((ds, dz, dx, (part - dz - dx) % SIDE))
    return listed


def finder():
    sec, z, x, y = place()

    def turned(at, size):
        return [at] + [lax.rem(at + step, size) for step in range(1, size)]

    secs, zs, xs, ys = turned(sec, 2), turned(z, SIDE), turned(x, SIDE), turned(y, SIDE)
    planes, lines = [v * (SIDE * SIDE) for v in zs], [v * SIDE for v in xs]

    def find(ds, dz, dx, dy):
        return secs[ds % 2], planes[dz % SIDE] + lines[dx % SIDE] + ys[dy % SIDE]

    return find


def layer_kernel(
    tok_ref,
    routes_ref,
    gate_ref,
    shard_ref,
    attn_gain_ref,
    kv_gain_ref,
    table_ref,
    length_ref,
    w_gate,
    w_up,
    w_down,
    queries,
    pool,
    out_ref,
    latent_ref,
    ctx_ref,
    sent,
    got,
    served,
    back,
    wg,
    wu,
    wd,
    hid,
    rows_buf,
    q_buf,
    pages,
    mixed,
    tops,
    sums,
    fresh,
    wz,
    normed_buf,
    normed_got,
    part_buf,
    part_got,
    load_sem,
    sent_sem,
    got_sem,
    served_sem,
    back_sem,
    wz_sent,
    wz_got,
    swap_sent,
    swap_got,
):
    sec, z, x, y = place()
    find = finder()
    order = offsets(SIDE)
    peers = len(order)
    tok_rows, width = tok_ref.shape
    parts = got_sem.shape[0]
    per_part = peers // parts
    quarter = peers // SIDE
    rows_q = quarter * CAP

    barrier = pltpu.get_barrier_semaphore()
    for offset in order[1:]:
        pl.semaphore_signal(barrier, inc=1, device_id=find(*offset), device_id_type=MESH)

    loads = [
        pltpu.make_async_copy(src, dst, load_sem.at[n])
        for n, (src, dst) in enumerate(
            (
                (queries, q_buf),
                (pool, pages),
                (w_gate.at[0], wg),
                (w_up.at[0], wu),
                (w_down.at[0], wd),
            )
        )
    ]
    for load in loads:
        load.start()

    row = lax.broadcasted_iota(jnp.int32, (1, peers * CAP), 1)
    j, c = row >> 1, row & 1
    ds, dz, dx, part = j & 1, (j >> 1) & 3, (j >> 3) & 3, j >> 5
    dy = (part - dz - dx) & 3
    expert = ((sec + ds) & 1) * (peers // 2) + ((z + dz) & 3) * 16 + ((x + dx) & 3) * 4 + ((y + dy) & 3)
    named = jnp.zeros((tok_rows, peers * CAP), jnp.float32)
    gates = jnp.zeros((tok_rows, peers * CAP), jnp.float32)
    for k in range(routes_ref.shape[1]):
        hit = routes_ref[:, k : k + 1] == expert
        named = jnp.where(hit, 1.0, named)
        gates = jnp.where(hit, gate_ref[:, k : k + 1].astype(jnp.float32), gates)
    earlier = (
        lax.broadcasted_iota(jnp.int32, (tok_rows, tok_rows), 1)
        < lax.broadcasted_iota(jnp.int32, (tok_rows, tok_rows), 0)
    ).astype(jnp.float32)
    before = jnp.dot(earlier, named, preferred_element_type=jnp.float32)
    in_slot = before == c.astype(jnp.float32)
    pick = jnp.where(in_slot, named, 0.0).astype(jnp.bfloat16)
    weigh = (jnp.where(in_slot, gates, 0.0) * (1.0 / GATE_DEN)).astype(jnp.bfloat16)

    for q in range(SIDE):
        gathered = lax.dot_general(
            pick[:, q * rows_q : (q + 1) * rows_q],
            tok_ref[...],
            (((0,), (0,)), ((), ())),
            preferred_element_type=jnp.float32,
        ).astype(jnp.bfloat16)
        sent[q * quarter : (q + 1) * quarter] = gathered.reshape(quarter, CAP, width)
    mine = pl.ds(3 * sec, 2 * LANE_TILES)
    wz[x, y, mine] = shard_ref[mine]

    pl.semaphore_wait(barrier, peers - 1)

    def push(src, dst, src_sem, dst_sem, offset):
        pltpu.make_async_remote_copy(
            src_ref=src,
            dst_ref=dst,
            send_sem=src_sem,
            recv_sem=dst_sem,
            device_id=find(*offset),
            device_id_type=MESH,
        ).start()

    def took(view, sem):
        pltpu.make_async_copy(view, view, sem).wait()

    def exchange(src, dst, src_sem, dst_sem, q, sign):
        for n in range(q * quarter, (q + 1) * quarter):
            if n == 0:
                pltpu.make_async_copy(src.at[0], dst.at[0], dst_sem).start()
            else:
                push(src.at[n], dst.at[n], src_sem, dst_sem, [sign * o for o in order[n]])

    lane_a = pl.ds(3 * sec, LANE_TILES)
    lane_b = pl.ds(3 * sec + LANE_TILES, LANE_TILES)
    other = pl.ds(4 * sec, 3)
    for step in range(1, SIDE):
        view = wz.at[x, y, lane_a]
        push(view, view, wz_sent.at[0], wz_got.at[0], (0, 0, step, 0))
        view = wz.at[x, y, lane_b]
        push(view, view, wz_sent.at[0], wz_got.at[1], (0, 0, 0, step))

    for q in range(2):
        exchange(sent, got, sent_sem, got_sem.at[q * parts // SIDE], q, 1)

    one = wz.at[pl.ds(0, 3), 0, pl.ds(0, LANE_TILES)]
    four = wz.at[pl.ds(0, 3), :, pl.ds(0, LANE_TILES)]
    took(one, wz_got.at[0])
    took(one, wz_got.at[1])
    for step in range(1, SIDE):
        view = wz.at[:, y, lane_a]
        push(view, view, wz_sent.at[1], wz_got.at[2], (0, 0, 0, step))
        view = wz.at[x, :, lane_b]
        push(view, view, wz_sent.at[1], wz_got.at[3], (0, 0, step, 0))

    for q in range(2, SIDE):
        exchange(sent, got, sent_sem, got_sem.at[q * parts // SIDE], q, 1)

    heads, kdim = q_buf.shape[1:]
    lat_width = mixed.shape[2]
    page = pages.shape[1]
    per_row = table_ref.shape[1]
    span = per_row * page
    loads[0].wait()
    loads[1].wait()

    def attend(t, c):
        keys = jnp.concatenate([pages[table_ref[t, i]] for i in range(per_row)], axis=0)
        scores = lax.dot_general(
            q_buf[t], keys, (((1,), (1,)), ((), ())), preferred_element_type=jnp.float32
        )
        kept = lax.broadcasted_iota(jnp.int32, (heads, span), 1) < length_ref[0, t]
        scores = jnp.where(kept, scores * score_scale, -1e30)
        top = jnp.max(scores, axis=1, keepdims=True)
        raised = jnp.where(kept, jnp.exp(scores - top), 0.0)
        tops[t] = top
        sums[t] = jnp.sum(raised, axis=1, keepdims=True)
        mixed[t] = jnp.dot(
            raised.astype(jnp.bfloat16), keys[:, :lat_width], preferred_element_type=jnp.float32
        )
        return c

    lax.fori_loop(0, tok_rows, attend, 0, unroll=2)

    took(four, wz_got.at[2])
    took(four, wz_got.at[3])
    view = wz.at[:, :, other]
    push(view, view, wz_sent.at[2], wz_got.at[4], (1, 0, 0, 0))

    for load in loads[2:]:
        load.wait()

    hidden = wg.shape[1]
    tile_h, tile_o = 256, 512
    for p in range(parts):
        took(got.at[pl.ds(p * per_part, per_part)], got_sem.at[p])
        rows_buf[...] = got[p * per_part : (p + 1) * per_part].reshape(per_part * CAP, width)

        def up(n, c):
            cols = pl.ds(pl.multiple_of(n * tile_h, tile_h), tile_h)
            g = jnp.dot(rows_buf[...], wg[:, cols], preferred_element_type=jnp.float32)
            u = jnp.dot(rows_buf[...], wu[:, cols], preferred_element_type=jnp.float32)
            hid[:, cols] = (g / (1.0 + jnp.exp(-g)) * u).astype(jnp.bfloat16)
            return c

        lax.fori_loop(0, hidden // tile_h, up, 0)

        def down(n, c, p=p):
            cols = pl.ds(pl.multiple_of(n * tile_o, tile_o), tile_o)
            o = jnp.dot(hid[...], wd[:, cols], preferred_element_type=jnp.float32)
            served[p * per_part : (p + 1) * per_part, :, cols] = o.astype(jnp.bfloat16).reshape(
                per_part, CAP, tile_o
            )
            return c

        lax.fori_loop(0, width // tile_o, down, 0)
        for q in range(p * SIDE // parts, (p + 1) * SIDE // parts):
            exchange(served, back, served_sem, back_sem, q, -1)

    took(wz.at[:, :, pl.ds(0, 3)], wz_got.at[4])
    took(back, back_sem)
    total = tok_ref[...].astype(jnp.float32)
    for q in range(SIDE):
        piece = back[q * quarter : (q + 1) * quarter].reshape(rows_q, width)
        total += jnp.dot(weigh[:, q * rows_q : (q + 1) * rows_q], piece, preferred_element_type=jnp.float32)
    layer_out = total.astype(jnp.bfloat16)
    out_ref[...] = layer_out

    normed = rms_scale(layer_out.astype(jnp.float32), attn_gain_ref[...]).astype(jnp.bfloat16)
    share = width // SIDE
    for m in range(SIDE):
        normed_buf[m] = normed[:, m * share : (m + 1) * share]
    zs = [z] + [lax.rem(z + step, SIDE) for step in range(1, SIDE)]
    for step in range(1, SIDE):
        push(normed_buf.at[zs[step]], normed_got.at[z], swap_sent.at[0], swap_got.at[0], (0, step, 0, 0))
    normed_got[z] = normed_buf[z]
    took(normed_got.at[pl.ds(0, SIDE - 1)], swap_got.at[0])
    partial = jnp.dot(
        normed_got[...].reshape(SIDE * tok_rows, share),
        wz[...].reshape(share, kdim),
        preferred_element_type=jnp.float32,
    )
    part_buf[...] = partial.reshape(SIDE, tok_rows, kdim)
    for step in range(1, SIDE):
        push(part_buf.at[zs[step]], part_got.at[z], swap_sent.at[1], swap_got.at[1], (0, step, 0, 0))
    part_got[z] = part_buf[z]
    took(part_got.at[pl.ds(0, SIDE - 1)], swap_got.at[1])
    latent_full = part_got[0] + part_got[1] + part_got[2] + part_got[3]
    latent = rms_scale(latent_full[:, :lat_width], kv_gain_ref[...])
    new_latent = jnp.concatenate([latent, latent_full[:, lat_width:]], axis=1).astype(jnp.bfloat16)
    latent_ref[...] = new_latent

    fresh[...] = lax.dot_general(
        q_buf[...].reshape(tok_rows * heads, kdim),
        new_latent,
        (((1,), (1,)), ((), ())),
        preferred_element_type=jnp.float32,
    ).reshape(tok_rows, heads, tok_rows)

    for t in range(tok_rows):
        score = fresh[t][:, t : t + 1] * score_scale
        top = jnp.maximum(tops[t], score)
        old, new = jnp.exp(tops[t] - top), jnp.exp(score - top)
        scale = 1.0 / (sums[t] * old + new)
        value = new_latent[t : t + 1, :lat_width].astype(jnp.float32)
        ctx_ref[t] = (mixed[t] * (old * scale) + (new * scale) * value).astype(jnp.bfloat16)

    took(sent.at[pl.ds(1, peers - 1)], sent_sem)
    took(served.at[pl.ds(1, peers - 1)], served_sem)
    took(wz.at[pl.ds(0, 3), pl.ds(0, 2), pl.ds(0, LANE_TILES)], wz_sent.at[0])
    took(wz.at[:, pl.ds(0, 3), pl.ds(0, 2 * LANE_TILES)], wz_sent.at[1])
    took(wz.at[:, :, pl.ds(0, 3)], wz_sent.at[2])
    took(normed_buf.at[pl.ds(0, SIDE - 1)], swap_sent.at[0])
    took(part_buf.at[pl.ds(0, SIDE - 1)], swap_sent.at[1])


def per_device(
    tokens,
    routes,
    gate_num,
    w_gate,
    w_up,
    w_down,
    attn_gain,
    w_latent,
    kv_gain,
    queries,
    cache_pool,
    block_table,
    lengths,
):
    peers = lax.axis_size("sec") * lax.axis_size("dev")
    tok_rows, width = tokens.shape
    hidden = w_gate.shape[2]
    heads, kdim = queries.shape[1:]
    lat_width = kv_gain.shape[0]
    tiles = w_latent.shape[0] // 8
    share = width // SIDE
    bf16, f32 = jnp.bfloat16, jnp.float32
    slots = pltpu.VMEM((peers, CAP, width), bf16)
    rows = peers * CAP // CHUNKS
    dma = pltpu.SemaphoreType.DMA
    vmem, smem = pl.BlockSpec(memory_space=pltpu.VMEM), pl.BlockSpec(memory_space=pltpu.SMEM)
    layer_out, new_latent, context = pl.pallas_call(
        layer_kernel,
        out_shape=(
            jax.ShapeDtypeStruct((tok_rows, width), bf16),
            jax.ShapeDtypeStruct((tok_rows, kdim), bf16),
            jax.ShapeDtypeStruct((tok_rows, heads, lat_width), bf16),
        ),
        in_specs=[vmem] * 6 + [smem] * 2 + [pl.BlockSpec(memory_space=pl.ANY)] * 5,
        out_specs=(vmem, vmem, vmem),
        scratch_shapes=[
            slots,
            slots,
            slots,
            slots,
            pltpu.VMEM((width, hidden), bf16),
            pltpu.VMEM((width, hidden), bf16),
            pltpu.VMEM((hidden, width), bf16),
            pltpu.VMEM((rows, hidden), bf16),
            pltpu.VMEM((rows, width), bf16),
            pltpu.VMEM(queries.shape, bf16),
            pltpu.VMEM(cache_pool.shape, bf16),
            pltpu.VMEM((tok_rows, heads, lat_width), f32),
            pltpu.VMEM((tok_rows, heads, 1), f32),
            pltpu.VMEM((tok_rows, heads, 1), f32),
            pltpu.VMEM((tok_rows, heads, tok_rows), f32),
            pltpu.VMEM((SIDE, SIDE, tiles, 8, kdim), bf16),
            pltpu.VMEM((SIDE, tok_rows, share), bf16),
            pltpu.VMEM((SIDE, tok_rows, share), bf16),
            pltpu.VMEM((SIDE, tok_rows, kdim), f32),
            pltpu.VMEM((SIDE, tok_rows, kdim), f32),
            dma((5,)),
            dma,
            dma((CHUNKS,)),
            dma,
            dma,
            dma((3,)),
            dma((5,)),
            dma((2,)),
            dma((2,)),
        ],
        compiler_params=pltpu.CompilerParams(
            collective_id=0, has_side_effects=True, vmem_limit_bytes=60 << 20
        ),
    )(
        tokens,
        routes,
        gate_num,
        w_latent.reshape(tiles, 8, kdim),
        attn_gain[None],
        kv_gain[None],
        block_table,
        lengths,
        w_gate,
        w_up,
        w_down,
        queries,
        cache_pool,
    )
    return (layer_out, new_latent, context.reshape(tok_rows, -1))


def solution(mesh):
    both = ("sec", "dev")
    return jax.shard_map(
        per_device,
        mesh=mesh,
        in_specs=(
            P(both, None),
            P(both, None),
            P(both, None),
            P(both, None, None),
            P(both, None, None),
            P(both, None, None),
            P(),
            P("dev", None),
            P(),
            P(both, None, None),
            P(both, None, None),
            P(both, None),
            P(both, None),
        ),
        out_specs=(P(both, None), P(both, None), P(both, None)),
        check_vma=False,
    )
```

```python
import functools

import jax
import jax.numpy as jnp
from jax import lax
from jax.experimental import pallas as pl
from jax.experimental.pallas import tpu as pltpu
from jax.sharding import PartitionSpec as P

MESH = pl.DeviceIdType.MESH
GATE_DEN = 32
CAP = 2
SIDE = 4
score_scale = 192.0 ** (-0.5)
norm_eps = 1e-06
CHUNKS = 4
LANE_TILES = 2


def rms_scale(values, gain):
    mean_square = jnp.mean(values * values, axis=-1, keepdims=True)
    return values * lax.rsqrt(mean_square + norm_eps) * gain


def place():
    sec, dev = lax.axis_index("sec"), lax.axis_index("dev")
    z = lax.div(dev, SIDE * SIDE)
    x = lax.rem(lax.div(dev, SIDE), SIDE)
    y = lax.rem(dev, SIDE)
    return sec, z, x, y


def offsets(parts):
    listed = []
    for part in range(parts):
        for i in range(2 * SIDE * SIDE):
            ds, dz, dx = i % 2, i // 2 % SIDE, i // (2 * SIDE)
            listed.append((ds, dz, dx, (part - dz - dx) % SIDE))
    return listed


def far_first(numbers, order):
    return sorted(numbers, key=lambda n: -sum(min(o, SIDE - o) for o in order[n][1:]) if n else 1)


def finder():
    sec, z, x, y = place()

    def turned(at, size):
        return [at] + [lax.rem(at + step, size) for step in range(1, size)]

    secs, zs, xs, ys = turned(sec, 2), turned(z, SIDE), turned(x, SIDE), turned(y, SIDE)
    planes, lines = [v * (SIDE * SIDE) for v in zs], [v * SIDE for v in xs]

    def find(ds, dz, dx, dy):
        return secs[ds % 2], planes[dz % SIDE] + lines[dx % SIDE] + ys[dy % SIDE]

    return find


def layer_kernel(
    tok_ref,
    routes_ref,
    gate_ref,
    shard_ref,
    attn_gain_ref,
    kv_gain_ref,
    table_ref,
    length_ref,
    w_gate,
    w_up,
    w_down,
    queries,
    pool,
    out_ref,
    latent_ref,
    ctx_ref,
    sent,
    got,
    served,
    back,
    wg,
    wu,
    wd,
    hid,
    rows_buf,
    q_buf,
    pages,
    mixed,
    tops,
    sums,
    wz,
    normed_buf,
    normed_got,
    part_buf,
    part_got,
    load_sem,
    sent_sem,
    got_sem,
    served_sem,
    back_sem,
    wz_sent,
    wz_got,
    swap_sent,
    swap_got,
):
    sec, z, x, y = place()
    find = finder()
    order = offsets(SIDE)
    peers = len(order)
    tok_rows, width = tok_ref.shape
    parts = got_sem.shape[0]
    per_part = peers // parts
    quarter = peers // SIDE
    rows_q = quarter * CAP

    barrier = pltpu.get_barrier_semaphore()
    for offset in order[1:]:
        pl.semaphore_signal(barrier, inc=1, device_id=find(*offset), device_id_type=MESH)

    loads = [
        pltpu.make_async_copy(src, dst, load_sem.at[n])
        for n, (src, dst) in enumerate(
            (
                (queries, q_buf),
                (pool, pages),
                (w_gate.at[0], wg),
                (w_up.at[0], wu),
                (w_down.at[0], wd),
            )
        )
    ]
    for load in loads:
        load.start()

    row = lax.broadcasted_iota(jnp.int32, (1, peers * CAP), 1)
    j, c = row >> 1, row & 1
    ds, dz, dx, part = j & 1, (j >> 1) & 3, (j >> 3) & 3, j >> 5
    dy = (part - dz - dx) & 3
    expert = ((sec + ds) & 1) * (peers // 2) + ((z + dz) & 3) * 16 + ((x + dx) & 3) * 4 + ((y + dy) & 3)
    named = jnp.zeros((tok_rows, peers * CAP), jnp.float32)
    gates = jnp.zeros((tok_rows, peers * CAP), jnp.float32)
    routes, gate_num = routes_ref[...].astype(jnp.float32).T, gate_ref[...].astype(jnp.float32).T
    expert = expert.astype(jnp.float32)
    for k in range(routes.shape[1]):
        hit = routes[:, k : k + 1] == expert
        named = jnp.where(hit, 1.0, named)
        gates = jnp.where(hit, gate_num[:, k : k + 1], gates)
    earlier = (
        lax.broadcasted_iota(jnp.int32, (tok_rows, tok_rows), 1)
        < lax.broadcasted_iota(jnp.int32, (tok_rows, tok_rows), 0)
    ).astype(jnp.float32)
    before = jnp.dot(earlier, named, preferred_element_type=jnp.float32)
    in_slot = before == c.astype(jnp.float32)
    pick = jnp.where(in_slot, named, 0.0).astype(jnp.bfloat16)
    weigh = (jnp.where(in_slot, gates, 0.0) * (1.0 / GATE_DEN)).astype(jnp.bfloat16)

    for q in range(SIDE):
        gathered = lax.dot_general(
            pick[:, q * rows_q : (q + 1) * rows_q],
            tok_ref[...],
            (((0,), (0,)), ((), ())),
            preferred_element_type=jnp.float32,
        ).astype(jnp.bfloat16)
        sent[q * quarter : (q + 1) * quarter] = gathered.reshape(quarter, CAP, width)
    mine = pl.ds(3 * sec, 2 * LANE_TILES)
    wz[x, y, mine] = shard_ref[mine]

    pl.semaphore_wait(barrier, peers - 1)

    def push(src, dst, src_sem, dst_sem, offset):
        pltpu.make_async_remote_copy(
            src_ref=src,
            dst_ref=dst,
            send_sem=src_sem,
            recv_sem=dst_sem,
            device_id=find(*offset),
            device_id_type=MESH,
        ).start()

    def took(view, sem):
        pltpu.make_async_copy(view, view, sem).wait()

    def exchange(src, dst, src_sem, dst_sem, q, sign):
        for n in far_first(range(q * quarter, (q + 1) * quarter), order):
            if n == 0:
                pltpu.make_async_copy(src.at[0], dst.at[0], dst_sem).start()
            else:
                push(src.at[n], dst.at[n], src_sem, dst_sem, [sign * o for o in order[n]])

    lane_a = pl.ds(3 * sec, LANE_TILES)
    lane_b = pl.ds(3 * sec + LANE_TILES, LANE_TILES)
    other = pl.ds(4 * sec, 3)
    for step in range(1, SIDE):
        view = wz.at[x, y, lane_a]
        push(view, view, wz_sent.at[0], wz_got.at[0], (0, 0, step, 0))
        view = wz.at[x, y, lane_b]
        push(view, view, wz_sent.at[0], wz_got.at[1], (0, 0, 0, step))

    for q in range(2):
        exchange(sent, got, sent_sem, got_sem.at[q * parts // SIDE], q, 1)

    one = wz.at[pl.ds(0, 3), 0, pl.ds(0, LANE_TILES)]
    four = wz.at[pl.ds(0, 3), :, pl.ds(0, LANE_TILES)]
    took(one, wz_got.at[0])
    took(one, wz_got.at[1])
    for step in range(1, SIDE):
        view = wz.at[:, y, lane_a]
        push(view, view, wz_sent.at[1], wz_got.at[2], (0, 0, 0, step))
        view = wz.at[x, :, lane_b]
        push(view, view, wz_sent.at[1], wz_got.at[3], (0, 0, step, 0))

    for q in range(2, SIDE):
        exchange(sent, got, sent_sem, got_sem.at[q * parts // SIDE], q, 1)

    heads, kdim = q_buf.shape[1:]
    lat_width = mixed.shape[2]
    page = pages.shape[1]
    per_row = table_ref.shape[0]
    span = per_row * page
    loads[0].wait()
    loads[1].wait()

    def attend(t, c):
        keys = jnp.concatenate([pages[table_ref[i, t]] for i in range(per_row)], axis=0)
        scores = lax.dot_general(
            keys, q_buf[t], (((1,), (1,)), ((), ())), preferred_element_type=jnp.float32
        )
        kept = lax.broadcasted_iota(jnp.int32, (span, heads), 0) < length_ref[0, t]
        scores = jnp.where(kept, scores * score_scale, -1e30)
        top = jnp.max(scores, axis=0, keepdims=True)
        raised = jnp.where(kept, jnp.exp(scores - top), 0.0)
        tops[t] = top
        sums[t] = jnp.sum(raised, axis=0, keepdims=True)
        mixed[t] = lax.dot_general(
            raised.astype(jnp.bfloat16),
            keys[:, :lat_width],
            (((0,), (0,)), ((), ())),
            preferred_element_type=jnp.float32,
        )
        return c

    lax.fori_loop(0, tok_rows, attend, 0, unroll=2)

    took(four, wz_got.at[2])
    took(four, wz_got.at[3])
    view = wz.at[:, :, other]
    push(view, view, wz_sent.at[2], wz_got.at[4], (1, 0, 0, 0))

    for load in loads[2:]:
        load.wait()

    hidden = wg.shape[1]
    tile_h, tile_o = 256, 512
    for p in range(parts):
        took(got.at[pl.ds(p * per_part, per_part)], got_sem.at[p])
        rows_buf[...] = got[p * per_part : (p + 1) * per_part].reshape(per_part * CAP, width)

        def up(n, c):
            cols = pl.ds(pl.multiple_of(n * tile_h, tile_h), tile_h)
            g = jnp.dot(rows_buf[...], wg[:, cols], preferred_element_type=jnp.float32)
            u = jnp.dot(rows_buf[...], wu[:, cols], preferred_element_type=jnp.float32)
            hid[:, cols] = (g / (1.0 + jnp.exp(-g)) * u).astype(jnp.bfloat16)
            return c

        lax.fori_loop(0, hidden // tile_h, up, 0)

        def down(n, c, p=p):
            cols = pl.ds(pl.multiple_of(n * tile_o, tile_o), tile_o)
            o = jnp.dot(hid[...], wd[:, cols], preferred_element_type=jnp.float32)
            served[p * per_part : (p + 1) * per_part, :, cols] = o.astype(jnp.bfloat16).reshape(
                per_part, CAP, tile_o
            )
            return c

        lax.fori_loop(0, width // tile_o, down, 0)
        for q in range(p * SIDE // parts, (p + 1) * SIDE // parts):
            exchange(served, back, served_sem, back_sem, q, -1)

    took(wz.at[:, :, pl.ds(0, 3)], wz_got.at[4])
    took(back, back_sem)
    total = tok_ref[...].astype(jnp.float32)
    for q in range(SIDE):
        piece = back[q * quarter : (q + 1) * quarter].reshape(rows_q, width)
        total += jnp.dot(weigh[:, q * rows_q : (q + 1) * rows_q], piece, preferred_element_type=jnp.float32)
    layer_out = total.astype(jnp.bfloat16)
    out_ref[...] = layer_out

    normed = rms_scale(layer_out.astype(jnp.float32), attn_gain_ref[...][None]).astype(jnp.bfloat16)
    share = width // SIDE
    for m in range(SIDE):
        normed_buf[m] = normed[:, m * share : (m + 1) * share]
    zs = [z] + [lax.rem(z + step, SIDE) for step in range(1, SIDE)]
    for step in range(1, SIDE):
        push(normed_buf.at[zs[step]], normed_got.at[z], swap_sent.at[0], swap_got.at[0], (0, step, 0, 0))
    normed_got[z] = normed_buf[z]
    took(normed_got.at[pl.ds(0, SIDE - 1)], swap_got.at[0])
    partial = jnp.dot(
        normed_got[...].reshape(SIDE * tok_rows, share),
        wz[...].reshape(share, kdim),
        preferred_element_type=jnp.float32,
    )
    part_buf[...] = partial.reshape(SIDE, tok_rows, kdim)
    for step in range(1, SIDE):
        push(part_buf.at[zs[step]], part_got.at[z], swap_sent.at[1], swap_got.at[1], (0, step, 0, 0))
    part_got[z] = part_buf[z]
    took(part_got.at[pl.ds(0, SIDE - 1)], swap_got.at[1])
    latent_full = part_got[0] + part_got[1] + part_got[2] + part_got[3]
    latent = rms_scale(latent_full[:, :lat_width], kv_gain_ref[...])
    new_latent = jnp.concatenate([latent, latent_full[:, lat_width:]], axis=1).astype(jnp.bfloat16)
    latent_ref[...] = new_latent

    against = lax.dot_general(
        new_latent,
        q_buf[...].reshape(tok_rows * heads, kdim),
        (((1,), (1,)), ((), ())),
        preferred_element_type=jnp.float32,
    )
    own = [against[t : t + 1, t * heads : (t + 1) * heads] for t in range(tok_rows)]
    score = jnp.concatenate(own, axis=0) * score_scale
    top_old = jnp.concatenate([tops[t] for t in range(tok_rows)], axis=0)
    sum_old = jnp.concatenate([sums[t] for t in range(tok_rows)], axis=0)
    top = jnp.maximum(top_old, score)
    old, new = jnp.exp(top_old - top), jnp.exp(score - top)
    scale = 1.0 / (sum_old * old + new)
    old, new = old * scale, new * scale
    value = new_latent[:, :lat_width].astype(jnp.float32)
    for h in range(heads):
        ctx_ref[:, h * lat_width : (h + 1) * lat_width] = (
            mixed[:, h, :] * old[:, h : h + 1] + value * new[:, h : h + 1]
        ).astype(jnp.bfloat16)

    took(sent.at[pl.ds(1, peers - 1)], sent_sem)
    took(served.at[pl.ds(1, peers - 1)], served_sem)
    took(wz.at[pl.ds(0, 3), pl.ds(0, 2), pl.ds(0, LANE_TILES)], wz_sent.at[0])
    took(wz.at[:, pl.ds(0, 3), pl.ds(0, 2 * LANE_TILES)], wz_sent.at[1])
    took(wz.at[:, :, pl.ds(0, 3)], wz_sent.at[2])
    took(normed_buf.at[pl.ds(0, SIDE - 1)], swap_sent.at[0])
    took(part_buf.at[pl.ds(0, SIDE - 1)], swap_sent.at[1])


def emit_kernel(a_ref, b_ref, c_ref, a_out, b_out, c_out, sem):
    pairs = ((a_ref, a_out), (b_ref, b_out), (c_ref, c_out))
    copies = [pltpu.make_async_copy(src, dst, sem.at[n]) for n, (src, dst) in enumerate(pairs)]
    for copy in copies:
        copy.start()
    for copy in copies:
        copy.wait()


def per_device(
    tokens,
    routes,
    gate_num,
    w_gate,
    w_up,
    w_down,
    attn_gain,
    w_latent,
    kv_gain,
    queries,
    cache_pool,
    block_table,
    lengths,
):
    peers = lax.axis_size("sec") * lax.axis_size("dev")
    tok_rows, width = tokens.shape
    hidden = w_gate.shape[2]
    heads, kdim = queries.shape[1:]
    lat_width = kv_gain.shape[0]
    tiles = w_latent.shape[0] // 8
    share = width // SIDE
    bf16, f32 = jnp.bfloat16, jnp.float32
    slots = pltpu.VMEM((peers, CAP, width), bf16)
    rows = peers * CAP // CHUNKS
    dma = pltpu.SemaphoreType.DMA
    vmem, smem = pl.BlockSpec(memory_space=pltpu.VMEM), pl.BlockSpec(memory_space=pltpu.SMEM)
    layer_out, new_latent, context = pl.pallas_call(
        layer_kernel,
        out_shape=(
            jax.ShapeDtypeStruct((tok_rows, width), bf16),
            jax.ShapeDtypeStruct((tok_rows, kdim), bf16),
            jax.ShapeDtypeStruct((tok_rows, heads * lat_width), bf16),
        ),
        in_specs=[vmem] * 6 + [smem] * 2 + [pl.BlockSpec(memory_space=pl.ANY)] * 5,
        out_specs=(vmem, vmem, vmem),
        scratch_shapes=[
            slots,
            slots,
            slots,
            slots,
            pltpu.VMEM((width, hidden), bf16),
            pltpu.VMEM((width, hidden), bf16),
            pltpu.VMEM((hidden, width), bf16),
            pltpu.VMEM((rows, hidden), bf16),
            pltpu.VMEM((rows, width), bf16),
            pltpu.VMEM(queries.shape, bf16),
            pltpu.VMEM(cache_pool.shape, bf16),
            pltpu.VMEM((tok_rows, heads, lat_width), f32),
            pltpu.VMEM((tok_rows, 1, heads), f32),
            pltpu.VMEM((tok_rows, 1, heads), f32),
            pltpu.VMEM((SIDE, SIDE, tiles, 8, kdim), bf16),
            pltpu.VMEM((SIDE, tok_rows, share), bf16),
            pltpu.VMEM((SIDE, tok_rows, share), bf16),
            pltpu.VMEM((SIDE, tok_rows, kdim), f32),
            pltpu.VMEM((SIDE, tok_rows, kdim), f32),
            dma((5,)),
            dma,
            dma((CHUNKS,)),
            dma,
            dma,
            dma((3,)),
            dma((5,)),
            dma((2,)),
            dma((2,)),
        ],
        compiler_params=pltpu.CompilerParams(
            collective_id=0, has_side_effects=True, vmem_limit_bytes=60 << 20
        ),
    )(
        tokens,
        routes.T,
        gate_num.T,
        w_latent.reshape(tiles, 8, kdim),
        attn_gain,
        kv_gain[None],
        block_table.T,
        lengths,
        w_gate,
        w_up,
        w_down,
        queries,
        cache_pool,
    )
    results = (layer_out, new_latent, context)
    anywhere = pl.BlockSpec(memory_space=pl.ANY)
    return pl.pallas_call(
        emit_kernel,
        out_shape=tuple(jax.ShapeDtypeStruct(v.shape, v.dtype) for v in results),
        in_specs=[anywhere] * 3,
        out_specs=(vmem,) * 3,
        scratch_shapes=[dma((3,))],
    )(*results)


def solution(mesh):
    both = ("sec", "dev")
    return jax.shard_map(
        per_device,
        mesh=mesh,
        in_specs=(
            P(both, None),
            P(both, None),
            P(both, None),
            P(both, None, None),
            P(both, None, None),
            P(both, None, None),
            P(),
            P("dev", None),
            P(),
            P(both, None, None),
            P(both, None, None),
            P(both, None),
            P(both, None),
        ),
        out_specs=(P(both, None), P(both, None), P(both, None)),
        check_vma=False,
    )
```

```python
import functools

import jax
import jax.numpy as jnp
from jax import lax
from jax.experimental import pallas as pl
from jax.experimental.pallas import tpu as pltpu
from jax.sharding import PartitionSpec as P

MESH = pl.DeviceIdType.MESH
GATE_DEN = 32
CAP = 2
SIDE = 4
score_scale = 192.0 ** (-0.5)
norm_eps = 1e-06
CHUNKS = 4
LANE_TILES = 2


def rms_scale(values, gain):
    mean_square = jnp.mean(values * values, axis=-1, keepdims=True)
    return values * lax.rsqrt(mean_square + norm_eps) * gain


def place():
    sec, dev = lax.axis_index("sec"), lax.axis_index("dev")
    z = lax.div(dev, SIDE * SIDE)
    x = lax.rem(lax.div(dev, SIDE), SIDE)
    y = lax.rem(dev, SIDE)
    return sec, z, x, y


def offsets(parts):
    listed = []
    for ring in range(2 * SIDE * SIDE):
        part, ds, dx = ring // (2 * SIDE), ring % 2, ring // 2 % SIDE
        listed += [(ds, dz, dx, (part - dx) % SIDE) for dz in range(SIDE)]
    return listed


def mixed_ways(numbers, order):
    numbers = list(numbers)
    return [numbers[(13 * i + 7) % len(numbers)] for i in range(len(numbers))]


def far_first(numbers, order):
    return sorted(numbers, key=lambda n: -sum(min(o, SIDE - o) for o in order[n][1:]) if n else 1)


def finder():
    sec, z, x, y = place()

    def turned(at, size):
        return [at] + [lax.rem(at + step, size) for step in range(1, size)]

    secs, zs, xs, ys = turned(sec, 2), turned(z, SIDE), turned(x, SIDE), turned(y, SIDE)
    planes, lines = [v * (SIDE * SIDE) for v in zs], [v * SIDE for v in xs]

    def find(ds, dz, dx, dy):
        return secs[ds % 2], planes[dz % SIDE] + lines[dx % SIDE] + ys[dy % SIDE]

    return find


def slot_table(routes, gate_num, expert, slot):
    tok_rows = routes.shape[0]
    named = jnp.zeros((tok_rows, expert.shape[1]), jnp.float32)
    gates = jnp.zeros((tok_rows, expert.shape[1]), jnp.float32)
    for k in range(routes.shape[1]):
        hit = routes[:, k : k + 1] == expert
        named = jnp.where(hit, 1.0, named)
        gates = jnp.where(hit, gate_num[:, k : k + 1], gates)
    earlier = (
        lax.broadcasted_iota(jnp.int32, (tok_rows, tok_rows), 1)
        < lax.broadcasted_iota(jnp.int32, (tok_rows, tok_rows), 0)
    ).astype(jnp.float32)
    before = jnp.dot(earlier, named, preferred_element_type=jnp.float32)
    in_slot = before == slot
    pick = jnp.where(in_slot, named, 0.0).astype(jnp.bfloat16)
    weigh = (jnp.where(in_slot, gates, 0.0) * (1.0 / GATE_DEN)).astype(jnp.bfloat16)
    return pick, weigh


def layer_kernel(
    tok_in,
    routes_in,
    gate_in,
    shard_in,
    attn_gain_in,
    kv_gain_in,
    table_in,
    length_in,
    w_gate,
    w_up,
    w_down,
    queries,
    pool,
    out_ref,
    latent_ref,
    ctx_ref,
    tok_ref,
    routes_ref,
    gate_ref,
    shard_ref,
    attn_gain_ref,
    kv_gain_ref,
    table_ref,
    length_ref,
    small_sem,
    sent,
    got,
    served,
    back,
    wg,
    wu,
    wd,
    hid,
    rows_buf,
    q_buf,
    pages,
    mixed,
    tops,
    sums,
    wz,
    tok_split,
    ring_tok,
    control,
    ring_control,
    ring_weigh,
    gain_split,
    moe_sum,
    lo_buf,
    lo_got,
    part_buf,
    part_got,
    load_sem,
    sent_sem,
    got_sem,
    served_sem,
    back_sem,
    wz_sent,
    wz_got,
    ring_sent,
    ring_got,
    swap_sent,
    swap_got,
):
    sec, z, x, y = place()
    find = finder()
    order = offsets(SIDE)
    peers = len(order)
    tok_rows, width = tok_ref.shape
    parts = got_sem.shape[0]
    per_part = peers // parts
    quarter = peers // SIDE
    rows_q = quarter * CAP

    barrier = pltpu.get_barrier_semaphore()
    for offset in order[1:]:
        pl.semaphore_signal(barrier, inc=1, device_id=find(*offset), device_id_type=MESH)

    smalls = [
        pltpu.make_async_copy(src, dst, small_sem.at[n])
        for n, (src, dst) in enumerate(
            (
                (routes_in, routes_ref),
                (gate_in, gate_ref),
                (tok_in, tok_ref),
                (shard_in, shard_ref),
                (attn_gain_in, attn_gain_ref),
                (kv_gain_in, kv_gain_ref),
                (table_in, table_ref),
                (length_in, length_ref),
            )
        )
    ]
    for small in smalls:
        small.start()
    loads = [
        pltpu.make_async_copy(src, dst, load_sem.at[n])
        for n, (src, dst) in enumerate(
            (
                (queries, q_buf),
                (pool, pages),
                (w_gate.at[0], wg),
                (w_up.at[0], wu),
                (w_down.at[0], wd),
            )
        )
    ]
    for load in loads:
        load.start()

    for small in smalls:
        small.wait()

    row = lax.broadcasted_iota(jnp.int32, (1, peers * CAP), 1)
    slot, dz, ds, dx = (row & 1).astype(jnp.float32), (row >> 1) & 3, (row >> 3) & 1, (row >> 4) & 3
    dy = ((row >> 6) - dx) & 3
    in_plane = ((sec + ds) & 1) * (peers // 2) + ((x + dx) & 3) * 4 + ((y + dy) & 3)
    routes, gate_num = routes_ref[...].astype(jnp.float32), gate_ref[...].astype(jnp.float32)
    expert = (in_plane + ((z + dz) & 3) * 16).astype(jnp.float32)
    pick, _ = slot_table(routes.T, gate_num.T, expert, slot)

    def build(q):
        gathered = lax.dot_general(
            pick[:, q * rows_q : (q + 1) * rows_q],
            tok_ref[...],
            (((0,), (0,)), ((), ())),
            preferred_element_type=jnp.float32,
        ).astype(jnp.bfloat16)
        sent[q * quarter : (q + 1) * quarter] = gathered.reshape(quarter, CAP, width)

    build(0)
    mine = pl.ds(3 * sec, 2 * LANE_TILES)
    wz[x, y, mine] = shard_ref[mine]
    control[0] = routes
    control[1] = gate_num
    share = width // SIDE
    for m in range(SIDE):
        tok_split[m] = tok_ref[:, m * share : (m + 1) * share]

    pl.semaphore_wait(barrier, peers - 1)

    def push(src, dst, src_sem, dst_sem, offset):
        pltpu.make_async_remote_copy(
            src_ref=src,
            dst_ref=dst,
            send_sem=src_sem,
            recv_sem=dst_sem,
            device_id=find(*offset),
            device_id_type=MESH,
        ).start()

    def took(view, sem):
        pltpu.make_async_copy(view, view, sem).wait()

    zs = [z] + [lax.rem(z + step, SIDE) for step in range(1, SIDE)]
    per_ring = quarter // SIDE

    def dispatch(q):
        for n in mixed_ways(range(q * quarter, (q + 1) * quarter), order):
            target = got.at[n // SIDE, z]
            if n == 0:
                pltpu.make_async_copy(sent.at[0], target, got_sem.at[0]).start()
            else:
                push(sent.at[n], target, sent_sem, got_sem.at[q], order[n])

    def give_back(q):
        for n in far_first(range(q * quarter, (q + 1) * quarter), order):
            ds, step, dx, dy = order[n]
            source, target = served.at[zs[step], n // SIDE], back.at[n // SIDE, z]
            if n == 0:
                pltpu.make_async_copy(source, target, back_sem.at[0]).start()
            else:
                push(source, target, served_sem, back_sem.at[q], (-ds, step, -dx, -dy))

    lane_a = pl.ds(3 * sec, LANE_TILES)
    lane_b = pl.ds(3 * sec + LANE_TILES, LANE_TILES)
    other = pl.ds(4 * sec, 3)
    for step in range(1, SIDE):
        view = wz.at[x, y, lane_a]
        push(view, view, wz_sent.at[0], wz_got.at[0], (0, 0, step, 0))
        view = wz.at[x, y, lane_b]
        push(view, view, wz_sent.at[0], wz_got.at[1], (0, 0, 0, step))

    dispatch(0)
    for step in range(1, SIDE):
        push(control, ring_control.at[z], ring_sent.at[0], ring_got.at[0], (0, step, 0, 0))
        push(tok_split.at[zs[step]], ring_tok.at[z], ring_sent.at[1], ring_got.at[1], (0, step, 0, 0))
    build(1)
    dispatch(1)
    one = wz.at[pl.ds(0, 3), 0, pl.ds(0, LANE_TILES)]
    four = wz.at[pl.ds(0, 3), :, pl.ds(0, LANE_TILES)]
    took(one, wz_got.at[0])
    took(one, wz_got.at[1])
    for step in range(1, SIDE):
        view = wz.at[:, y, lane_a]
        push(view, view, wz_sent.at[1], wz_got.at[2], (0, 0, 0, step))
        view = wz.at[x, :, lane_b]
        push(view, view, wz_sent.at[1], wz_got.at[3], (0, 0, step, 0))

    build(2)
    dispatch(2)
    build(3)
    dispatch(3)

    ring_control[z] = control[...]
    ring_tok[z] = tok_split[z]
    gain = attn_gain_ref[...][None]
    for m in range(SIDE):
        gain_split[m] = gain[:, m * share : (m + 1) * share]
    took(ring_control.at[pl.ds(0, SIDE - 1)], ring_got.at[0])
    expert = (in_plane + dz * 16).astype(jnp.float32)
    for m in range(SIDE):
        ring_weigh[m] = slot_table(ring_control[m, 0].T, ring_control[m, 1].T, expert, slot)[1]

    heads, kdim = q_buf.shape[1:]
    lat_width = mixed.shape[2]
    page = pages.shape[1]
    per_row = table_ref.shape[0]
    span = per_row * page
    loads[0].wait()
    loads[1].wait()

    def attend(t, c):
        keys = jnp.concatenate([pages[table_ref[i, t]] for i in range(per_row)], axis=0)
        scores = lax.dot_general(
            keys, q_buf[t], (((1,), (1,)), ((), ())), preferred_element_type=jnp.float32
        )
        kept = lax.broadcasted_iota(jnp.int32, (span, heads), 0) < length_ref[0, t]
        scores = jnp.where(kept, scores * score_scale, -1e30)
        top = jnp.max(scores, axis=0, keepdims=True)
        raised = jnp.where(kept, jnp.exp(scores - top), 0.0)
        tops[t] = top
        sums[t] = jnp.sum(raised, axis=0, keepdims=True)
        mixed[t] = lax.dot_general(
            raised.astype(jnp.bfloat16),
            keys[:, :lat_width],
            (((0,), (0,)), ((), ())),
            preferred_element_type=jnp.float32,
        )
        return c

    lax.fori_loop(0, 8, attend, 0, unroll=2)


    for load in loads[2:]:
        load.wait()

    hidden = wg.shape[1]
    tile_h = 256
    for p in range(parts):
        rings = pl.ds(p * per_ring, per_ring)
        took(got.at[rings], got_sem.at[p])
        rows_buf[...] = got[rings].reshape(rows_q, width)

        def up(n, c):
            cols = pl.ds(pl.multiple_of(n * tile_h, tile_h), tile_h)
            g = jnp.dot(rows_buf[...], wg[:, cols], preferred_element_type=jnp.float32)
            u = jnp.dot(rows_buf[...], wu[:, cols], preferred_element_type=jnp.float32)
            hid[:, cols] = (g / (1.0 + jnp.exp(-g)) * u).astype(jnp.bfloat16)
            return c

        lax.fori_loop(0, hidden // tile_h, up, 0)

        def down(m, c, rings=rings):
            cols = pl.ds(pl.multiple_of(m * share, share), share)
            o = jnp.dot(hid[...], wd[:, cols], preferred_element_type=jnp.float32)
            served[m, rings] = o.astype(jnp.bfloat16).reshape(per_ring, SIDE, CAP, share)
            return c

        lax.fori_loop(0, SIDE, down, 0)
        give_back(p)
        if p == 1:
            took(four, wz_got.at[2])
            took(four, wz_got.at[3])
            view = wz.at[:, :, other]
            push(view, view, wz_sent.at[2], wz_got.at[4], (1, 0, 0, 0))
        if p == parts - 1:
            lax.fori_loop(8, 16, attend, 0, unroll=2)

    took(wz.at[:, :, pl.ds(0, 3)], wz_got.at[4])
    took(ring_tok.at[pl.ds(0, SIDE - 1)], ring_got.at[1])

    for p in range(parts):
        rings = pl.ds(p * per_ring, per_ring)
        took(back.at[rings], back_sem.at[p])
        for m in range(SIDE):
            piece = back[rings, :, m].reshape(rows_q, share)
            base = ring_tok[m].astype(jnp.float32) if p == 0 else moe_sum[m]
            moe_sum[m] = base + jnp.dot(
                ring_weigh[m, :, p * rows_q : (p + 1) * rows_q], piece, preferred_element_type=jnp.float32
            )
    layer_out = moe_sum[...].astype(jnp.bfloat16)
    lo_buf[...] = layer_out
    wide = layer_out.astype(jnp.float32)
    squares = jnp.sum(wide * wide, axis=-1, keepdims=True)
    scaled = (wide * gain_split[z][None]).astype(jnp.bfloat16)
    partial = jnp.dot(
        scaled.reshape(SIDE * tok_rows, share),
        wz[...].reshape(share, kdim),
        preferred_element_type=jnp.float32,
    ).reshape(SIDE, tok_rows, kdim)
    part_buf[:, :, :kdim] = partial
    part_buf[:, :, kdim:] = jnp.broadcast_to(squares, (SIDE, tok_rows, part_buf.shape[2] - kdim))
    for step in range(1, SIDE):
        push(part_buf.at[zs[step]], part_got.at[z], swap_sent.at[1], swap_got.at[1], (0, step, 0, 0))
    for step in range(1, SIDE):
        push(lo_buf.at[zs[step]], lo_got.at[z], swap_sent.at[0], swap_got.at[0], (0, step, 0, 0))
    part_got[z] = part_buf[z]
    lo_got[z] = lo_buf[z]
    took(part_got.at[pl.ds(0, SIDE - 1)], swap_got.at[1])
    whole = part_got[0] + part_got[1] + part_got[2] + part_got[3]
    latent_full = whole[:, :kdim] * lax.rsqrt(whole[:, kdim : kdim + 1] / width + norm_eps)
    latent = rms_scale(latent_full[:, :lat_width], kv_gain_ref[...])
    new_latent = jnp.concatenate([latent, latent_full[:, lat_width:]], axis=1).astype(jnp.bfloat16)
    latent_ref[...] = new_latent

    against = lax.dot_general(
        new_latent,
        q_buf[...].reshape(tok_rows * heads, kdim),
        (((1,), (1,)), ((), ())),
        preferred_element_type=jnp.float32,
    )
    own = [against[t : t + 1, t * heads : (t + 1) * heads] for t in range(tok_rows)]
    score = jnp.concatenate(own, axis=0) * score_scale
    top_old = jnp.concatenate([tops[t] for t in range(tok_rows)], axis=0)
    sum_old = jnp.concatenate([sums[t] for t in range(tok_rows)], axis=0)
    top = jnp.maximum(top_old, score)
    old, new = jnp.exp(top_old - top), jnp.exp(score - top)
    scale = 1.0 / (sum_old * old + new)
    old, new = old * scale, new * scale
    value = new_latent[:, :lat_width].astype(jnp.float32)
    for h in range(heads):
        ctx_ref[:, h * lat_width : (h + 1) * lat_width] = (
            mixed[:, h, :] * old[:, h : h + 1] + value * new[:, h : h + 1]
        ).astype(jnp.bfloat16)

    took(lo_got.at[pl.ds(0, SIDE - 1)], swap_got.at[0])
    for m in range(SIDE):
        out_ref[:, m * share : (m + 1) * share] = lo_got[m]

    took(sent.at[pl.ds(1, peers - 1)], sent_sem)
    took(served.at[pl.ds(0, SIDE - 1)], served_sem)
    took(served.at[0, pl.ds(1, peers // SIDE - 1)], served_sem)
    took(wz.at[pl.ds(0, 3), pl.ds(0, 2), pl.ds(0, LANE_TILES)], wz_sent.at[0])
    took(wz.at[:, pl.ds(0, 3), pl.ds(0, 2 * LANE_TILES)], wz_sent.at[1])
    took(wz.at[:, :, pl.ds(0, 3)], wz_sent.at[2])
    took(ring_control.at[pl.ds(0, SIDE - 1)], ring_sent.at[0])
    took(tok_split.at[pl.ds(0, SIDE - 1)], ring_sent.at[1])
    took(lo_buf.at[pl.ds(0, SIDE - 1)], swap_sent.at[0])
    took(part_buf.at[pl.ds(0, SIDE - 1)], swap_sent.at[1])


def emit_kernel(a_ref, b_ref, c_ref, a_out, b_out, c_out, sem):
    pairs = ((a_ref, a_out), (b_ref, b_out), (c_ref, c_out))
    copies = [pltpu.make_async_copy(src, dst, sem.at[n]) for n, (src, dst) in enumerate(pairs)]
    for copy in copies:
        copy.start()
    for copy in copies:
        copy.wait()


def per_device(
    tokens,
    routes,
    gate_num,
    w_gate,
    w_up,
    w_down,
    attn_gain,
    w_latent,
    kv_gain,
    queries,
    cache_pool,
    block_table,
    lengths,
):
    peers = lax.axis_size("sec") * lax.axis_size("dev")
    tok_rows, width = tokens.shape
    hidden = w_gate.shape[2]
    heads, kdim = queries.shape[1:]
    lat_width = kv_gain.shape[0]
    tiles = w_latent.shape[0] // 8
    share = width // SIDE
    bf16, f32 = jnp.bfloat16, jnp.float32
    rings = peers // SIDE
    rows = peers * CAP // CHUNKS
    dma = pltpu.SemaphoreType.DMA
    vmem, smem = pl.BlockSpec(memory_space=pltpu.VMEM), pl.BlockSpec(memory_space=pltpu.SMEM)
    layer_out, new_latent, context = pl.pallas_call(
        layer_kernel,
        out_shape=(
            jax.ShapeDtypeStruct((tok_rows, width), bf16),
            jax.ShapeDtypeStruct((tok_rows, kdim), bf16),
            jax.ShapeDtypeStruct((tok_rows, heads * lat_width), bf16),
        ),
        in_specs=[pl.BlockSpec(memory_space=pl.ANY)] * 13,
        out_specs=(vmem, vmem, vmem),
        scratch_shapes=[
            pltpu.VMEM((tok_rows, width), bf16),
            pltpu.VMEM(routes.shape[::-1], jnp.int32),
            pltpu.VMEM(gate_num.shape[::-1], jnp.int32),
            pltpu.VMEM((tiles, 8, kdim), bf16),
            pltpu.VMEM(attn_gain.shape, f32),
            pltpu.VMEM((1, lat_width), f32),
            pltpu.SMEM(block_table.shape[::-1], jnp.int32),
            pltpu.SMEM(lengths.shape, jnp.int32),
            dma((8,)),
            pltpu.VMEM((peers, CAP, width), bf16),
            pltpu.VMEM((rings, SIDE, CAP, width), bf16),
            pltpu.VMEM((SIDE, rings, SIDE, CAP, share), bf16),
            pltpu.VMEM((rings, SIDE, SIDE, CAP, share), bf16),
            pltpu.VMEM((width, hidden), bf16),
            pltpu.VMEM((width, hidden), bf16),
            pltpu.VMEM((hidden, width), bf16),
            pltpu.VMEM((rows, hidden), bf16),
            pltpu.VMEM((rows, width), bf16),
            pltpu.VMEM(queries.shape, bf16),
            pltpu.VMEM(cache_pool.shape, bf16),
            pltpu.VMEM((tok_rows, heads, lat_width), f32),
            pltpu.VMEM((tok_rows, 1, heads), f32),
            pltpu.VMEM((tok_rows, 1, heads), f32),
            pltpu.VMEM((SIDE, SIDE, tiles, 8, kdim), bf16),
            pltpu.VMEM((SIDE, tok_rows, share), bf16),
            pltpu.VMEM((SIDE, tok_rows, share), bf16),
            pltpu.VMEM((2, routes.shape[1], tok_rows), f32),
            pltpu.VMEM((SIDE, 2, routes.shape[1], tok_rows), f32),
            pltpu.VMEM((SIDE, tok_rows, peers * CAP), bf16),
            pltpu.VMEM((SIDE, 1, share), f32),
            pltpu.VMEM((SIDE, tok_rows, share), f32),
            pltpu.VMEM((SIDE, tok_rows, share), bf16),
            pltpu.VMEM((SIDE, tok_rows, share), bf16),
            pltpu.VMEM((SIDE, tok_rows, kdim + 64), f32),
            pltpu.VMEM((SIDE, tok_rows, kdim + 64), f32),
            dma((5,)),
            dma,
            dma((CHUNKS,)),
            dma,
            dma((CHUNKS,)),
            dma((3,)),
            dma((5,)),
            dma((2,)),
            dma((2,)),
            dma((2,)),
            dma((2,)),
        ],
        compiler_params=pltpu.CompilerParams(
            collective_id=0, has_side_effects=True, vmem_limit_bytes=60 << 20
        ),
    )(
        tokens,
        routes.T,
        gate_num.T,
        w_latent.reshape(tiles, 8, kdim),
        attn_gain,
        kv_gain[None],
        block_table.T,
        lengths,
        w_gate,
        w_up,
        w_down,
        queries,
        cache_pool,
    )
    results = (layer_out, new_latent, context)
    anywhere = pl.BlockSpec(memory_space=pl.ANY)
    return pl.pallas_call(
        emit_kernel,
        out_shape=tuple(jax.ShapeDtypeStruct(v.shape, v.dtype) for v in results),
        in_specs=[anywhere] * 3,
        out_specs=(vmem,) * 3,
        scratch_shapes=[dma((3,))],
    )(*results)


def solution(mesh):
    both = ("sec", "dev")
    return jax.shard_map(
        per_device,
        mesh=mesh,
        in_specs=(
            P(both, None),
            P(both, None),
            P(both, None),
            P(both, None, None),
            P(both, None, None),
            P(both, None, None),
            P(),
            P("dev", None),
            P(),
            P(both, None, None),
            P(both, None, None),
            P(both, None),
            P(both, None),
        ),
        out_specs=(P(both, None), P(both, None), P(both, None)),
        check_vma=False,
    )
```

```python
import functools

import jax
import jax.numpy as jnp
from jax import lax
from jax.experimental import pallas as pl
from jax.experimental.pallas import tpu as pltpu
from jax.sharding import PartitionSpec as P

MESH = pl.DeviceIdType.MESH
GATE_DEN = 32
CAP = 2
SIDE = 4
score_scale = 192.0 ** (-0.5)
norm_eps = 1e-06
CHUNKS = 4
LANE_TILES = 2


def rms_scale(values, gain):
    mean_square = jnp.mean(values * values, axis=-1, keepdims=True)
    return values * lax.rsqrt(mean_square + norm_eps) * gain


def place():
    sec, dev = lax.axis_index("sec"), lax.axis_index("dev")
    z = lax.div(dev, SIDE * SIDE)
    x = lax.rem(lax.div(dev, SIDE), SIDE)
    y = lax.rem(dev, SIDE)
    return sec, z, x, y


def offsets(parts):
    listed = []
    for ring in range(2 * SIDE * SIDE):
        part, ds, dx = ring // (2 * SIDE), ring % 2, ring // 2 % SIDE
        listed += [(ds, dz, dx, (part - dx) % SIDE) for dz in range(SIDE)]
    return listed


def mixed_ways(numbers, order):
    numbers = list(numbers)
    return [numbers[(13 * i + 7) % len(numbers)] for i in range(len(numbers))]


def far_first(numbers, order):
    return sorted(numbers, key=lambda n: -sum(min(o, SIDE - o) for o in order[n][1:]) if n else 1)


def finder():
    sec, z, x, y = place()

    def turned(at, size):
        return [at] + [lax.rem(at + step, size) for step in range(1, size)]

    secs, zs, xs, ys = turned(sec, 2), turned(z, SIDE), turned(x, SIDE), turned(y, SIDE)
    planes, lines = [v * (SIDE * SIDE) for v in zs], [v * SIDE for v in xs]

    def find(ds, dz, dx, dy):
        return secs[ds % 2], planes[dz % SIDE] + lines[dx % SIDE] + ys[dy % SIDE]

    return find


def slot_table(routes, gate_num, expert, slot):
    tok_rows = routes.shape[0]
    named = jnp.zeros((tok_rows, expert.shape[1]), jnp.float32)
    gates = jnp.zeros((tok_rows, expert.shape[1]), jnp.float32)
    for k in range(routes.shape[1]):
        hit = routes[:, k : k + 1] == expert
        named = jnp.where(hit, 1.0, named)
        gates = jnp.where(hit, gate_num[:, k : k + 1], gates)
    earlier = (
        lax.broadcasted_iota(jnp.int32, (tok_rows, tok_rows), 1)
        < lax.broadcasted_iota(jnp.int32, (tok_rows, tok_rows), 0)
    ).astype(jnp.float32)
    before = jnp.dot(earlier, named, preferred_element_type=jnp.float32)
    in_slot = before == slot
    pick = jnp.where(in_slot, named, 0.0).astype(jnp.bfloat16)
    weigh = (jnp.where(in_slot, gates, 0.0) * (1.0 / GATE_DEN)).astype(jnp.bfloat16)
    return pick, weigh


def layer_kernel(
    tok_in,
    routes_in,
    gate_in,
    shard_in,
    attn_gain_in,
    kv_gain_in,
    table_in,
    length_in,
    w_gate,
    w_up,
    w_down,
    queries,
    pool,
    out_ref,
    latent_ref,
    ctx_out,
    ctx_ref,
    ctx_sem,
    tok_ref,
    routes_ref,
    gate_ref,
    shard_ref,
    attn_gain_ref,
    kv_gain_ref,
    table_ref,
    length_ref,
    small_sem,
    sent,
    got,
    served,
    back,
    wg,
    wu,
    wd,
    hid,
    rows_buf,
    q_buf,
    pages,
    mixed,
    tops,
    sums,
    wz,
    tok_split,
    ring_tok,
    control,
    ring_control,
    ring_weigh,
    gain_split,
    moe_sum,
    lo_buf,
    lo_got,
    part_buf,
    part_got,
    load_sem,
    sent_sem,
    got_sem,
    served_sem,
    back_sem,
    wz_sent,
    wz_got,
    ring_sent,
    ring_got,
    swap_sent,
    swap_got,
):
    sec, z, x, y = place()
    find = finder()
    order = offsets(SIDE)
    peers = len(order)
    tok_rows, width = tok_ref.shape
    parts = got_sem.shape[0]
    per_part = peers // parts
    quarter = peers // SIDE
    rows_q = quarter * CAP

    barrier = pltpu.get_barrier_semaphore()
    for offset in order[1:]:
        pl.semaphore_signal(barrier, inc=1, device_id=find(*offset), device_id_type=MESH)

    smalls = [
        pltpu.make_async_copy(src, dst, small_sem.at[n])
        for n, (src, dst) in enumerate(
            (
                (routes_in, routes_ref),
                (gate_in, gate_ref),
                (tok_in, tok_ref),
                (shard_in, shard_ref),
                (attn_gain_in, attn_gain_ref),
                (kv_gain_in, kv_gain_ref),
                (table_in, table_ref),
                (length_in, length_ref),
            )
        )
    ]
    for small in smalls:
        small.start()
    loads = [
        pltpu.make_async_copy(src, dst, load_sem.at[n])
        for n, (src, dst) in enumerate(
            (
                (queries, q_buf),
                (pool, pages),
                (w_gate.at[0], wg),
                (w_up.at[0], wu),
                (w_down.at[0], wd),
            )
        )
    ]
    for load in loads:
        load.start()

    for small in smalls:
        small.wait()

    row = lax.broadcasted_iota(jnp.int32, (1, peers * CAP), 1)
    slot, dz, ds, dx = (row & 1).astype(jnp.float32), (row >> 1) & 3, (row >> 3) & 1, (row >> 4) & 3
    dy = ((row >> 6) - dx) & 3
    in_plane = ((sec + ds) & 1) * (peers // 2) + ((x + dx) & 3) * 4 + ((y + dy) & 3)
    routes, gate_num = routes_ref[...].astype(jnp.float32), gate_ref[...].astype(jnp.float32)
    expert = (in_plane + ((z + dz) & 3) * 16).astype(jnp.float32)
    pick, _ = slot_table(routes.T, gate_num.T, expert, slot)

    def build(q):
        gathered = lax.dot_general(
            pick[:, q * rows_q : (q + 1) * rows_q],
            tok_ref[...],
            (((0,), (0,)), ((), ())),
            preferred_element_type=jnp.float32,
        ).astype(jnp.bfloat16)
        sent[q * quarter : (q + 1) * quarter] = gathered.reshape(quarter, CAP, width)

    build(0)
    mine = pl.ds(3 * sec, 2 * LANE_TILES)
    wz[x, y, mine] = shard_ref[mine]
    control[0] = routes
    control[1] = gate_num
    share = width // SIDE
    for m in range(SIDE):
        tok_split[m] = tok_ref[:, m * share : (m + 1) * share]

    pl.semaphore_wait(barrier, peers - 1)

    def push(src, dst, src_sem, dst_sem, offset):
        pltpu.make_async_remote_copy(
            src_ref=src,
            dst_ref=dst,
            send_sem=src_sem,
            recv_sem=dst_sem,
            device_id=find(*offset),
            device_id_type=MESH,
        ).start()

    def took(view, sem):
        pltpu.make_async_copy(view, view, sem).wait()

    zs = [z] + [lax.rem(z + step, SIDE) for step in range(1, SIDE)]
    per_ring = quarter // SIDE

    def dispatch(q):
        for n in mixed_ways(range(q * quarter, (q + 1) * quarter), order):
            target = got.at[n // SIDE, z]
            if n == 0:
                pltpu.make_async_copy(sent.at[0], target, got_sem.at[0]).start()
            else:
                push(sent.at[n], target, sent_sem, got_sem.at[q], order[n])

    def give_back(q):
        for n in far_first(range(q * quarter, (q + 1) * quarter), order):
            ds, step, dx, dy = order[n]
            source, target = served.at[zs[step], n // SIDE], back.at[n // SIDE, z]
            if n == 0:
                pltpu.make_async_copy(source, target, back_sem.at[0]).start()
            else:
                push(source, target, served_sem, back_sem.at[q], (-ds, step, -dx, -dy))

    lane_a = pl.ds(3 * sec, LANE_TILES)
    lane_b = pl.ds(3 * sec + LANE_TILES, LANE_TILES)
    other = pl.ds(4 * sec, 3)
    for step in range(1, SIDE):
        view = wz.at[x, y, lane_a]
        push(view, view, wz_sent.at[0], wz_got.at[0], (0, 0, step, 0))
        view = wz.at[x, y, lane_b]
        push(view, view, wz_sent.at[0], wz_got.at[1], (0, 0, 0, step))

    dispatch(0)
    for step in range(1, SIDE):
        push(control, ring_control.at[z], ring_sent.at[0], ring_got.at[0], (0, step, 0, 0))
        push(tok_split.at[zs[step]], ring_tok.at[z], ring_sent.at[1], ring_got.at[1], (0, step, 0, 0))
    build(1)
    dispatch(1)
    one = wz.at[pl.ds(0, 3), 0, pl.ds(0, LANE_TILES)]
    four = wz.at[pl.ds(0, 3), :, pl.ds(0, LANE_TILES)]
    took(one, wz_got.at[0])
    took(one, wz_got.at[1])
    build(2)
    dispatch(2)
    for step in range(1, SIDE):
        view = wz.at[:, y, lane_a]
        push(view, view, wz_sent.at[1], wz_got.at[2], (0, 0, 0, step))
        view = wz.at[x, :, lane_b]
        push(view, view, wz_sent.at[1], wz_got.at[3], (0, 0, step, 0))

    build(3)
    dispatch(3)

    ring_control[z] = control[...]
    ring_tok[z] = tok_split[z]
    gain = attn_gain_ref[...][None]
    for m in range(SIDE):
        gain_split[m] = gain[:, m * share : (m + 1) * share]
    took(ring_control.at[pl.ds(0, SIDE - 1)], ring_got.at[0])
    expert = (in_plane + dz * 16).astype(jnp.float32)
    for m in range(SIDE):
        ring_weigh[m] = slot_table(ring_control[m, 0].T, ring_control[m, 1].T, expert, slot)[1]

    heads, kdim = q_buf.shape[1:]
    lat_width = mixed.shape[2]
    page = pages.shape[1]
    per_row = table_ref.shape[0]
    span = per_row * page
    loads[0].wait()
    loads[1].wait()

    def attend(t, c):
        keys = jnp.concatenate([pages[table_ref[i, t]] for i in range(per_row)], axis=0)
        scores = lax.dot_general(
            keys, q_buf[t], (((1,), (1,)), ((), ())), preferred_element_type=jnp.float32
        )
        kept = lax.broadcasted_iota(jnp.int32, (span, heads), 0) < length_ref[0, t]
        scores = jnp.where(kept, scores * score_scale, -1e30)
        top = jnp.max(scores, axis=0, keepdims=True)
        raised = jnp.where(kept, jnp.exp(scores - top), 0.0)
        tops[t] = top
        sums[t] = jnp.sum(raised, axis=0, keepdims=True)
        mixed[t] = lax.dot_general(
            raised.astype(jnp.bfloat16),
            keys[:, :lat_width],
            (((0,), (0,)), ((), ())),
            preferred_element_type=jnp.float32,
        )
        return c

    lax.fori_loop(0, 8, attend, 0, unroll=2)


    for load in loads[2:]:
        load.wait()

    hidden = wg.shape[1]
    tile_h = 256
    for p in range(parts):
        rings = pl.ds(p * per_ring, per_ring)
        took(got.at[rings], got_sem.at[p])
        rows_buf[...] = got[rings].reshape(rows_q, width)

        def up(n, c):
            cols = pl.ds(pl.multiple_of(n * tile_h, tile_h), tile_h)
            g = jnp.dot(rows_buf[...], wg[:, cols], preferred_element_type=jnp.float32)
            u = jnp.dot(rows_buf[...], wu[:, cols], preferred_element_type=jnp.float32)
            hid[:, cols] = (g / (1.0 + jnp.exp(-g)) * u).astype(jnp.bfloat16)
            return c

        lax.fori_loop(0, hidden // tile_h, up, 0)

        def down(m, c, rings=rings):
            cols = pl.ds(pl.multiple_of(m * share, share), share)
            o = jnp.dot(hid[...], wd[:, cols], preferred_element_type=jnp.float32)
            served[m, rings] = o.astype(jnp.bfloat16).reshape(per_ring, SIDE, CAP, share)
            return c

        lax.fori_loop(0, SIDE, down, 0)
        give_back(p)
        if p == 1:
            took(four, wz_got.at[2])
            took(four, wz_got.at[3])
            view = wz.at[:, :, other]
            push(view, view, wz_sent.at[2], wz_got.at[4], (1, 0, 0, 0))
        if p == parts - 1:
            lax.fori_loop(8, 16, attend, 0, unroll=2)

    took(wz.at[:, :, pl.ds(0, 3)], wz_got.at[4])
    took(ring_tok.at[pl.ds(0, SIDE - 1)], ring_got.at[1])

    for p in range(parts):
        rings = pl.ds(p * per_ring, per_ring)
        took(back.at[rings], back_sem.at[p])
        for m in range(SIDE):
            piece = back[rings, :, m].reshape(rows_q, share)
            base = ring_tok[m].astype(jnp.float32) if p == 0 else moe_sum[m]
            moe_sum[m] = base + jnp.dot(
                ring_weigh[m, :, p * rows_q : (p + 1) * rows_q], piece, preferred_element_type=jnp.float32
            )
    layer_out = moe_sum[...].astype(jnp.bfloat16)
    lo_buf[...] = layer_out
    wide = layer_out.astype(jnp.float32)
    squares = jnp.sum(wide * wide, axis=-1, keepdims=True)
    scaled = (wide * gain_split[z][None]).astype(jnp.bfloat16)
    partial = jnp.dot(
        scaled.reshape(SIDE * tok_rows, share),
        wz[...].reshape(share, kdim),
        preferred_element_type=jnp.float32,
    ).reshape(SIDE, tok_rows, kdim)
    half = (part_buf.shape[2] - kdim) // 2
    coarse = squares.astype(jnp.bfloat16)
    fine = (squares - coarse.astype(jnp.float32)).astype(jnp.bfloat16)
    part_buf[:, :, :kdim] = partial.astype(jnp.bfloat16)
    part_buf[:, :, kdim : kdim + half] = jnp.broadcast_to(coarse, (SIDE, tok_rows, half))
    part_buf[:, :, kdim + half :] = jnp.broadcast_to(fine, (SIDE, tok_rows, half))
    for step in range(1, SIDE):
        push(part_buf.at[zs[step]], part_got.at[z], swap_sent.at[1], swap_got.at[1], (0, step, 0, 0))
    for step in range(1, SIDE):
        push(lo_buf.at[zs[step]], lo_got.at[z], swap_sent.at[0], swap_got.at[0], (0, step, 0, 0))
    part_got[z] = part_buf[z]
    lo_got[z] = lo_buf[z]
    took(part_got.at[pl.ds(0, SIDE - 1)], swap_got.at[1])
    whole = jnp.sum(part_got[...].astype(jnp.float32), axis=0)
    square_sum = whole[:, kdim : kdim + 1] + whole[:, kdim + half : kdim + half + 1]
    latent_full = whole[:, :kdim] * lax.rsqrt(square_sum / width + norm_eps)
    latent = rms_scale(latent_full[:, :lat_width], kv_gain_ref[...])
    new_latent = jnp.concatenate([latent, latent_full[:, lat_width:]], axis=1).astype(jnp.bfloat16)
    latent_ref[...] = new_latent

    against = lax.dot_general(
        new_latent,
        q_buf[...].reshape(tok_rows * heads, kdim),
        (((1,), (1,)), ((), ())),
        preferred_element_type=jnp.float32,
    )
    own = [against[t : t + 1, t * heads : (t + 1) * heads] for t in range(tok_rows)]
    score = jnp.concatenate(own, axis=0) * score_scale
    top_old = jnp.concatenate([tops[t] for t in range(tok_rows)], axis=0)
    sum_old = jnp.concatenate([sums[t] for t in range(tok_rows)], axis=0)
    top = jnp.maximum(top_old, score)
    old, new = jnp.exp(top_old - top), jnp.exp(score - top)
    scale = 1.0 / (sum_old * old + new)
    old, new = old * scale, new * scale
    value = new_latent[:, :lat_width].astype(jnp.float32)
    leaving = []
    batch = heads // ctx_sem.shape[0]
    for h in range(heads):
        ctx_ref[:, h * lat_width : (h + 1) * lat_width] = (
            mixed[:, h, :] * old[:, h : h + 1] + value * new[:, h : h + 1]
        ).astype(jnp.bfloat16)
        if h % batch == batch - 1:
            cols = pl.ds((h + 1 - batch) * lat_width, batch * lat_width)
            leaving.append(pltpu.make_async_copy(ctx_ref.at[:, cols], ctx_out.at[:, cols], ctx_sem.at[h // batch]))
            leaving[-1].start()

    took(lo_got.at[pl.ds(0, SIDE - 1)], swap_got.at[0])
    for m in range(SIDE):
        out_ref[:, m * share : (m + 1) * share] = lo_got[m]

    took(sent.at[pl.ds(1, peers - 1)], sent_sem)
    took(served.at[pl.ds(0, SIDE - 1)], served_sem)
    took(served.at[0, pl.ds(1, peers // SIDE - 1)], served_sem)
    took(wz.at[pl.ds(0, 3), pl.ds(0, 2), pl.ds(0, LANE_TILES)], wz_sent.at[0])
    took(wz.at[:, pl.ds(0, 3), pl.ds(0, 2 * LANE_TILES)], wz_sent.at[1])
    took(wz.at[:, :, pl.ds(0, 3)], wz_sent.at[2])
    took(ring_control.at[pl.ds(0, SIDE - 1)], ring_sent.at[0])
    took(tok_split.at[pl.ds(0, SIDE - 1)], ring_sent.at[1])
    took(lo_buf.at[pl.ds(0, SIDE - 1)], swap_sent.at[0])
    took(part_buf.at[pl.ds(0, SIDE - 1)], swap_sent.at[1])
    for copy in leaving:
        copy.wait()


def emit_kernel(a_ref, b_ref, c_ref, a_out, b_out, c_out, a_buf, b_buf, c_buf, in_sem, out_sem):
    trips = [(a_ref, a_buf, a_out), (b_ref, b_buf, b_out)]
    pieces = in_sem.shape[0] - len(trips)
    step = c_ref.shape[1] // pieces
    for i in range(pieces):
        cols = pl.ds(i * step, step)
        trips.append((c_ref.at[:, cols], c_buf.at[:, cols], c_out.at[:, cols]))
    comes = [pltpu.make_async_copy(src, buf, in_sem.at[n]) for n, (src, buf, _) in enumerate(trips)]
    goes = [pltpu.make_async_copy(buf, dst, out_sem.at[n]) for n, (_, buf, dst) in enumerate(trips)]
    for copy in comes:
        copy.start()
    for come, go in zip(comes, goes):
        come.wait()
        go.start()
    for copy in goes:
        copy.wait()


def per_device(
    tokens,
    routes,
    gate_num,
    w_gate,
    w_up,
    w_down,
    attn_gain,
    w_latent,
    kv_gain,
    queries,
    cache_pool,
    block_table,
    lengths,
):
    peers = lax.axis_size("sec") * lax.axis_size("dev")
    tok_rows, width = tokens.shape
    hidden = w_gate.shape[2]
    heads, kdim = queries.shape[1:]
    lat_width = kv_gain.shape[0]
    tiles = w_latent.shape[0] // 8
    share = width // SIDE
    bf16, f32 = jnp.bfloat16, jnp.float32
    rings = peers // SIDE
    rows = peers * CAP // CHUNKS
    dma = pltpu.SemaphoreType.DMA
    vmem, smem = pl.BlockSpec(memory_space=pltpu.VMEM), pl.BlockSpec(memory_space=pltpu.SMEM)
    layer_out, new_latent, context = pl.pallas_call(
        layer_kernel,
        out_shape=(
            jax.ShapeDtypeStruct((tok_rows, width), bf16),
            jax.ShapeDtypeStruct((tok_rows, kdim), bf16),
            jax.ShapeDtypeStruct((tok_rows, heads * lat_width), bf16),
        ),
        in_specs=[pl.BlockSpec(memory_space=pl.ANY)] * 13,
        out_specs=(vmem, vmem, pl.BlockSpec(memory_space=pl.ANY)),
        scratch_shapes=[
            pltpu.VMEM((tok_rows, heads * lat_width), bf16),
            dma((4,)),
            pltpu.VMEM((tok_rows, width), bf16),
            pltpu.VMEM(routes.shape[::-1], jnp.int32),
            pltpu.VMEM(gate_num.shape[::-1], jnp.int32),
            pltpu.VMEM((tiles, 8, kdim), bf16),
            pltpu.VMEM(attn_gain.shape, f32),
            pltpu.VMEM((1, lat_width), f32),
            pltpu.SMEM(block_table.shape[::-1], jnp.int32),
            pltpu.SMEM(lengths.shape, jnp.int32),
            dma((8,)),
            pltpu.VMEM((peers, CAP, width), bf16),
            pltpu.VMEM((rings, SIDE, CAP, width), bf16),
            pltpu.VMEM((SIDE, rings, SIDE, CAP, share), bf16),
            pltpu.VMEM((rings, SIDE, SIDE, CAP, share), bf16),
            pltpu.VMEM((width, hidden), bf16),
            pltpu.VMEM((width, hidden), bf16),
            pltpu.VMEM((hidden, width), bf16),
            pltpu.VMEM((rows, hidden), bf16),
            pltpu.VMEM((rows, width), bf16),
            pltpu.VMEM(queries.shape, bf16),
            pltpu.VMEM(cache_pool.shape, bf16),
            pltpu.VMEM((tok_rows, heads, lat_width), f32),
            pltpu.VMEM((tok_rows, 1, heads), f32),
            pltpu.VMEM((tok_rows, 1, heads), f32),
            pltpu.VMEM((SIDE, SIDE, tiles, 8, kdim), bf16),
            pltpu.VMEM((SIDE, tok_rows, share), bf16),
            pltpu.VMEM((SIDE, tok_rows, share), bf16),
            pltpu.VMEM((2, routes.shape[1], tok_rows), f32),
            pltpu.VMEM((SIDE, 2, routes.shape[1], tok_rows), f32),
            pltpu.VMEM((SIDE, tok_rows, peers * CAP), bf16),
            pltpu.VMEM((SIDE, 1, share), f32),
            pltpu.VMEM((SIDE, tok_rows, share), f32),
            pltpu.VMEM((SIDE, tok_rows, share), bf16),
            pltpu.VMEM((SIDE, tok_rows, share), bf16),
            pltpu.VMEM((SIDE, tok_rows, kdim + 64), bf16),
            pltpu.VMEM((SIDE, tok_rows, kdim + 64), bf16),
            dma((5,)),
            dma,
            dma((CHUNKS,)),
            dma,
            dma((CHUNKS,)),
            dma((3,)),
            dma((5,)),
            dma((2,)),
            dma((2,)),
            dma((2,)),
            dma((2,)),
        ],
        compiler_params=pltpu.CompilerParams(
            collective_id=0, has_side_effects=True, vmem_limit_bytes=60 << 20
        ),
    )(
        tokens,
        routes.T,
        gate_num.T,
        w_latent.reshape(tiles, 8, kdim),
        attn_gain,
        kv_gain[None],
        block_table.T,
        lengths,
        w_gate,
        w_up,
        w_down,
        queries,
        cache_pool,
    )
    results = (layer_out, new_latent, context)
    anywhere = pl.BlockSpec(memory_space=pl.ANY)
    return pl.pallas_call(
        emit_kernel,
        out_shape=tuple(jax.ShapeDtypeStruct(v.shape, v.dtype) for v in results),
        in_specs=[anywhere] * 3,
        out_specs=(anywhere,) * 3,
        scratch_shapes=[pltpu.VMEM(v.shape, v.dtype) for v in results] + [dma((6,)), dma((6,))],
    )(*results)


def solution(mesh):
    both = ("sec", "dev")
    return jax.shard_map(
        per_device,
        mesh=mesh,
        in_specs=(
            P(both, None),
            P(both, None),
            P(both, None),
            P(both, None, None),
            P(both, None, None),
            P(both, None, None),
            P(),
            P("dev", None),
            P(),
            P(both, None, None),
            P(both, None, None),
            P(both, None),
            P(both, None),
        ),
        out_specs=(P(both, None), P(both, None), P(both, None)),
        check_vma=False,
    )
```
